32 devices in a mesh: groups: 2 (over y), gx: 4 (over z), gy: 4 (over x, core).
Axes of the slice: x: 2, y: 2, z: 4, core: 2. Of those that a mesh axis runs over, the one named last changes fastest.
Arguments:
- children: float32 [4, 4, 4, 512, 512], P('groups', 'gx', 'gy'), parts along dimension 0, as said below
Outputs:
- merged: float32 [4, 4, 4, 256, 1024], P('groups', 'gx', 'gy'), parts along dimension 0
There are 2 independent parts, one for each index of `groups`. The reference program is written for one: setup_inputs(seed, part) draws one part's arguments, and reference() takes and returns one part's arrays. A program takes and returns all parts, laid end to end along the dimension named above; each array names one. Nothing has to cross between parts.
Inputs may be any that keep to these rules, and one draw needn't show every extreme that they name: `children`: every child operator is symmetric, and every sum S formed at either level is symmetric positive definite with smallest eigenvalue at least 1.
All inputs are finite; a program needn't handle non-finite values.
Results may differ from the reference program's by a relative error of at most 0.00005.
Values sent between devices are 32-bit elements; how exact they have to be, the bound alone decides.
No kernel may reach another device: no remote copies, remote signals or barrier semaphores. Data moves between devices by JAX's collectives and lax.ppermute only.
A program may use at most 64 MiB of HBM per device.

```python
import jax
import jax.numpy as jnp
import numpy as np
from jax import lax

SIDE = 128
WAVES = 2
BOXES_X = 4
BOXES_Y = 4


def draw_children(key, part):
    order_one = 4 * SIDE
    points = jnp.arange(order_one)
    sides = points // SIDE
    coords = ((points % SIDE).astype(jnp.float32) + 0.5) / SIDE
    xcoord = jnp.where(sides == 0, 0.0, jnp.where(sides == 1, 1.0, coords))
    ycoord = jnp.where(sides == 2, 0.0, jnp.where(sides == 3, 1.0, coords))
    distance = jnp.sqrt((xcoord[:, None] - xcoord[None, :]) ** 2 + (ycoord[:, None] - ycoord[None, :]) ** 2)
    kernel = jnp.exp(-distance / 0.5)
    key_scale, key_rough, key_diag = jax.random.split(jax.random.fold_in(key, 11), 3)
    shape = (WAVES, BOXES_X, BOXES_Y, order_one)
    scales = jax.random.uniform(key_scale, shape, jnp.float32, 0.3, 1.0)
    spread = 4.0 * order_one ** (-0.5)
    diagonal = jax.random.uniform(key_diag, shape, jnp.float32, 4.5, 6.0)
    rough = jax.random.uniform(key_rough, shape + (order_one,), jnp.float32, -spread, spread)
    rough = 0.5 * (rough + jnp.swapaxes(rough, -1, -2))
    result = scales[..., :, None] * scales[..., None, :] * kernel + rough
    result = result + diagonal[..., :, None] * jnp.eye(order_one, dtype=jnp.float32)
    return result.astype(jnp.float32)


def setup_inputs(seed: int = 0, part: int = 0) -> dict:
    streams_of = jax.random.split(jax.random.key(seed), 2)
    own_keys = jax.random.split(jax.random.fold_in(streams_of[1], part), 2)
    children = draw_children(jax.random.fold_in(jax.random.fold_in(streams_of[1], part), 71), part)
    return dict(children=children)


def side_blocks(order):
    return np.concatenate([np.arange(block * SIDE, (block + 1) * SIDE) for block in order])

def definite_solve(matrix, right_sides):
    factor = jnp.linalg.cholesky(matrix)
    return jax.scipy.linalg.cho_solve((factor, True), right_sides)

def merge_pair(first, second, ext_a, inner_a, ext_b, inner_b):
    schur = first[inner_a][:, inner_a] + second[inner_b][:, inner_b]
    right_sides = jnp.concatenate([first[inner_a][:, ext_a], second[inner_b][:, ext_b]], 1)
    solution_map = definite_solve(schur, right_sides)
    count_a = len(ext_a)
    count_b = len(ext_b)
    upper = jnp.concatenate([first[ext_a][:, ext_a], jnp.zeros((count_a, count_b), jnp.float32)], 1)
    lower = jnp.concatenate([jnp.zeros((count_b, count_a), jnp.float32), second[ext_b][:, ext_b]], 1)
    coupling = jnp.concatenate([first[ext_a][:, inner_a], second[ext_b][:, inner_b]], 0)
    return jnp.concatenate([upper, lower], 0) - jnp.dot(coupling, solution_map, precision=lax.Precision.HIGHEST)

def reference(children):
    order_one = 4 * SIDE
    half_y = BOXES_Y // 2
    half_x = BOXES_X // 2
    bottoms = children[:, :, :half_y].reshape(-1, order_one, order_one)
    tops = children[:, :, half_y:].reshape(-1, order_one, order_one)
    ext_a = side_blocks((0, 1, 2))
    inner_a = side_blocks((3,))
    ext_b = side_blocks((0, 1, 3))
    inner_b = side_blocks((2,))
    middle = lax.map(lambda pair: merge_pair(pair[0], pair[1], ext_a, inner_a, ext_b, inner_b), (bottoms, tops))
    middle = middle.reshape(WAVES, BOXES_X, half_y, 6 * SIDE, 6 * SIDE)
    lefts = middle[:, :half_x].reshape(-1, 6 * SIDE, 6 * SIDE)
    rights = middle[:, half_x:].reshape(-1, 6 * SIDE, 6 * SIDE)
    ext_l = side_blocks((0, 2, 3, 5))
    inner_l = side_blocks((1, 4))
    ext_r = side_blocks((1, 2, 4, 5))
    inner_r = side_blocks((0, 3))
    quads = lax.map(lambda pair: merge_pair(pair[0], pair[1], ext_l, inner_l, ext_r, inner_r), (lefts, rights))
    quads = quads.reshape(WAVES, half_x, half_y, 2, 2, 2 * SIDE, 8 * SIDE)
    quads = jnp.transpose(quads, (0, 3, 1, 4, 2, 5, 6))
    return quads.reshape(WAVES, BOXES_X, BOXES_Y, 2 * SIDE, 8 * SIDE)
```

```python
import functools

import jax
import jax.numpy as jnp
from jax import lax
from jax.experimental import pallas as pl
from jax.experimental.pallas import tpu as pltpu
from jax.sharding import PartitionSpec as P

SUB = 8


def swapped(block, axis):
    count = lax.axis_size(axis)
    bit = count.bit_length() - 2
    route = []
    for low in range(count):
        high = low | 1 << bit
        if high != low and high < count:
            route += [(low, high), (high, low)]
    return lax.ppermute(block, axis, route)


def after(block, other):
    return lax.optimization_barrier((block, other))[0]


def role():
    right = (lax.axis_index("gx") >= lax.axis_size("gx") // 2).astype(jnp.int32)
    top = (lax.axis_index("gy") >= lax.axis_size("gy") // 2).astype(jnp.int32)
    return right, top


def mul(a, b):
    return lax.dot_general(
        a, b, (((1,), (0,)), ((), ())), precision=lax.Precision.HIGHEST, preferred_element_type=jnp.float32
    )


def mul_t(a, b):
    return lax.dot_general(
        a, b, (((0,), (0,)), ((), ())), precision=lax.Precision.HIGHEST, preferred_element_type=jnp.float32
    )


def tree(terms):
    while len(terms) > 1:
        terms = [terms[i] + terms[i + 1] for i in range(0, len(terms) - 1, 2)] + terms[len(terms) & ~1 :]
    return terms[0]


def inverses(matrices):
    size = matrices[0].shape[0]
    panels = size // SUB
    many = len(matrices)
    lane = lax.broadcasted_iota(jnp.int32, (SUB, size), 1)
    sub = lax.broadcasted_iota(jnp.int32, (SUB, size), 0)
    full = lambda v: jnp.broadcast_to(v, (SUB, size))
    state = [[m[SUB * i : SUB * i + SUB, :] for i in range(panels)] for m in matrices]
    lower = [[] for _ in matrices]
    scaled = [[] for _ in matrices]
    for p in range(panels):
        first = SUB * p
        inside = (lane >= first) & (lane < first + SUB)
        unit = lane - first == sub
        done = lane < first + SUB
        blocks = [[full(state[w][p][:, first + j : first + j + 1]) for j in range(SUB)] for w in range(many)]
        for k in range(SUB):
            at_row = sub == k
            for w in range(many):
                old = blocks[w]
                pivot = old[k]
                inverse = 1.0 / full(pivot[k : k + 1, :])
                new = []
                for j in range(SUB):
                    if j == k:
                        new.append(jnp.where(at_row, inverse, -pivot * inverse))
                    else:
                        scaled_row = full(old[j][k : k + 1, :]) * inverse
                        new.append(jnp.where(at_row, scaled_row, old[j] - pivot * scaled_row))
                blocks[w] = new
        for w in range(many):
            rows = state[w]
            panel = jnp.where(inside, jnp.where(unit, 1.0, 0.0), rows[p])
            gained = tree([blocks[w][l] * full(panel[l : l + 1, :]) for l in range(SUB)])
            lower[w].append(jnp.where(done, panel, 0.0))
            scaled[w].append(jnp.where(done, gained, 0.0))
            spread = [full(gained[l : l + 1, :]) for l in range(SUB)]
            for i in range(p + 1, panels):
                row = rows[i]
                change = tree([full(row[:, first + l : first + l + 1]) * spread[l] for l in range(SUB)])
                rows[i] = jnp.where(inside, 0.0, row) - change
    return [mul_t(jnp.concatenate(lower[w], 0), jnp.concatenate(scaled[w], 0)) for w in range(many)]


def square_masks(side):
    row = lax.broadcasted_iota(jnp.int32, (side, side), 0)
    col = lax.broadcasted_iota(jnp.int32, (side, side), 1)
    return row > col, row == col


def pack_yy(square):
    below, diag = square_masks(square.shape[0])
    return jnp.where(below | diag, square, square.T)


def pack_xx(square, line):
    below, diag = square_masks(square.shape[0])
    return jnp.where(diag, jnp.broadcast_to(line, square.shape), jnp.where(below, square.T, square))


def interface_kernel(side, tiles, pack, own_yy, own_xx, sems):
    right, top = role()
    side_y = 3 - top
    side_x = 1 - right
    waves = pack.shape[0]

    def piece(w, row_side, col_side):
        rows = pl.ds(pl.multiple_of(row_side * side, side), side)
        cols = pl.ds(pl.multiple_of(col_side * side, side), side)
        return tiles.at[w, rows, cols]

    copies = []
    for w in range(waves):
        copies += [
            pltpu.make_async_copy(piece(w, side_y, side_y), own_yy.at[w], sems.at[3 * w]),
            pltpu.make_async_copy(piece(w, side_x, side_x), own_xx.at[w], sems.at[3 * w + 1]),
            pltpu.make_async_copy(piece(w, side_y, side_x), pack.at[w, pl.ds(side, side), :], sems.at[3 * w + 2]),
        ]
    for copy in copies:
        copy.start()
    below, diag = square_masks(side)
    for w in range(waves):
        copies[3 * w].wait()
        copies[3 * w + 1].wait()
        xx = own_xx[w]
        pack[w, 0:side, :] = jnp.where(below | diag, own_yy[w], xx)
        line = jnp.sum(jnp.where(diag, xx, 0.0), 0, keepdims=True)
        pack[w, 2 * side :, :] = jnp.broadcast_to(line, (SUB, side))
    for w in range(waves):
        copies[3 * w + 2].wait()


def interfaces(tiles):
    waves, side = tiles.shape[0], tiles.shape[1] // 4
    return pl.pallas_call(
        functools.partial(interface_kernel, side),
        name="interfaces",
        out_shape=jax.ShapeDtypeStruct((waves, 2 * side + SUB, side), jnp.float32),
        in_specs=[pl.BlockSpec(memory_space=pl.ANY)],
        out_specs=pl.BlockSpec(memory_space=pltpu.VMEM),
        scratch_shapes=[
            pltpu.VMEM((waves, side, side), jnp.float32),
            pltpu.VMEM((waves, side, side), jnp.float32),
            pltpu.SemaphoreType.DMA((3 * waves,)),
        ],
        cost_estimate=pl.CostEstimate(flops=0, bytes_accessed=5 * waves * side * side * 4, transcendentals=0),
    )(tiles)


def coupling_kernel(side, tiles, whole, first, second, third, sems):
    right, top = role()
    rows_of = (3 - top, 1 - right)
    cols_of = (right, 2 + top)
    copies = []
    for w in range(2):
        for i in range(2):
            rows = pl.ds(pl.multiple_of(rows_of[i] * side, side), side)
            here = pl.ds(i * side, side)
            for j in range(2):
                cols = pl.ds(pl.multiple_of(cols_of[j] * side, side), side)
                source = tiles.at[w, rows, cols]
                there = pl.ds(j * side, side)
                n = len(copies)
                copies.append(pltpu.make_async_copy(source, whole.at[w, here, there], sems.at[n]))
                if w == 0:
                    target = first.at[here, there]
                else:
                    target = (second, third)[j].at[here, :]
                copies.append(pltpu.make_async_copy(source, target, sems.at[n + 1]))
    for copy in copies:
        copy.start()
    for copy in copies:
        copy.wait()


def couplings(tiles):
    waves, side = tiles.shape[0], tiles.shape[1] // 4
    shapes = [(waves, 2 * side, 2 * side), (2 * side, 2 * side), (2 * side, side), (2 * side, side)]
    return pl.pallas_call(
        functools.partial(coupling_kernel, side),
        name="couplings",
        out_shape=[jax.ShapeDtypeStruct(s, jnp.float32) for s in shapes],
        in_specs=[pl.BlockSpec(memory_space=pl.ANY)],
        out_specs=[pl.BlockSpec(memory_space=pltpu.VMEM)] * 4,
        scratch_shapes=[pltpu.SemaphoreType.DMA((8 * waves,))],
        cost_estimate=pl.CostEstimate(flops=0, bytes_accessed=16 * waves * side * side * 4, transcendentals=0),
    )(tiles)


def first_kernel(side, own, mate, coupling, blocks, sides):
    waves = own.shape[0]
    sums = [pack_yy(own[w, 0:side, :] + mate[w, 0:side, :]) for w in range(waves)]
    inverse = inverses(sums)
    for w in range(waves):
        own_yx = own[w, side : 2 * side, :]
        mate_yu = mate[w, side : 2 * side, :]
        gain_x = mul(inverse[w], own_yx)
        gain_u = mul(inverse[w], mate_yu)
        blocks[w, 0] = gain_x
        blocks[w, 1] = gain_u
        blocks[w, 2] = pack_xx(own[w, 0:side, :], own[w, 2 * side : 2 * side + 1, :]) - mul_t(own_yx, gain_x)
        blocks[w, 3] = -mul_t(own_yx, gain_u)
        blocks[w, 4] = pack_xx(mate[w, 0:side, :], mate[w, 2 * side : 2 * side + 1, :]) - mul_t(mate_yu, gain_u)
        side_y = coupling[w, 0:side, :]
        sides[w, 0] = mul(inverse[w], side_y)
        sides[w, 1] = coupling[w, side:, :] - mul_t(gain_x, side_y)
        sides[w, 2] = -mul_t(gain_u, side_y)


def second_kernel(side, pack, one, sides_one, blocks, sides):
    waves = pack.shape[0]
    sums = [
        one[w, 2] + pack_xx(pack[w, 0:side, :], pack[w, 2 * side : 2 * side + 1, :]) for w in range(waves)
    ]
    inverse = inverses(sums)
    for w in range(waves):
        vx = pack[w, side : 2 * side, :]
        xu = one[w, 3]
        gain_v = mul(inverse[w], vx.T)
        gain_u = mul(inverse[w], xu)
        blocks[w, 0] = gain_v
        blocks[w, 1] = gain_u
        blocks[w, 2] = pack_yy(pack[w, 0:side, :]) - mul(vx, gain_v)
        blocks[w, 3] = -mul(vx, gain_u)
        blocks[w, 4] = one[w, 4] - mul_t(xu, gain_u)
        side_x = sides_one[w, 1]
        sides[w, 0] = mul(inverse[w], side_x)
        sides[w, 1] = -mul_t(gain_v, side_x)
        sides[w, 2] = sides_one[w, 2] - mul_t(gain_u, side_x)


def third_kernel(side, pack, one, sides_one, two, sides_two, held):
    waves = pack.shape[0]
    inverse_v = inverses([two[w, 2] + pack_yy(pack[w, 0:side, :]) for w in range(waves)])
    vu = [two[w, 3] + pack[w, side : 2 * side, :] for w in range(waves)]
    gain = [mul(inverse_v[w], vu[w]) for w in range(waves)]
    inverse_u = inverses(
        [
            two[w, 4]
            + pack_xx(pack[w, 0:side, :], pack[w, 2 * side : 2 * side + 1, :])
            - mul_t(vu[w], gain[w])
            for w in range(waves)
        ]
    )
    for w in range(waves):
        side_v = sides_two[w, 1]
        side_u = sides_two[w, 2] - mul_t(gain[w], side_v)
        held_u = mul(inverse_u[w], side_u)
        held_v = mul(inverse_v[w], side_v) - mul(gain[w], held_u)
        held_x = sides_two[w, 0] - mul(two[w, 0], held_v) - mul(two[w, 1], held_u)
        held_y = sides_one[w, 0] - mul(one[w, 0], held_x) - mul(one[w, 1], held_u)
        held[w, 0] = held_y
        held[w, 1] = held_x
        held[w, 2] = held_v
        held[w, 3] = held_u


def whole_call(kernel, name, shapes, flops):
    return lambda *args: pl.pallas_call(
        kernel,
        name=name,
        out_shape=[jax.ShapeDtypeStruct(s, jnp.float32) for s in shapes],
        in_specs=[pl.BlockSpec(memory_space=pltpu.VMEM)] * len(args),
        out_specs=[pl.BlockSpec(memory_space=pltpu.VMEM)] * len(shapes),
        compiler_params=pltpu.CompilerParams(vmem_limit_bytes=32 << 20),
        cost_estimate=pl.CostEstimate(flops=flops, bytes_accessed=1 << 20, transcendentals=0),
    )(*args)


def near_kernel(side, tiles, held, own, mate, cross, far, out, diagonal, buffer, load_sems, sems):
    right, top = role()
    sides = (right, 2 + top)
    loads = []
    for w in range(2):
        for i in range(2):
            rows = pl.ds(pl.multiple_of(sides[i] * side, side), side)
            for j in range(2):
                cols = pl.ds(pl.multiple_of(sides[j] * side, side), side)
                loads.append(
                    pltpu.make_async_copy(
                        tiles.at[w, rows, cols],
                        diagonal.at[w, pl.ds(i * side, side), pl.ds(j * side, side)],
                        load_sems.at[len(loads)],
                    )
                )
                loads[-1].start()
    stores = []

    def put(n, w, slot, value):
        buffer[n] = value
        column = pl.multiple_of(slot * 2 * side, 2 * side)
        stores.append(pltpu.make_async_copy(buffer.at[n], out.at[w, :, pl.ds(column, 2 * side)], sems.at[n]))
        stores[-1].start()

    mate_slot = 2 * right + 1 - top
    cross_slot = 2 * (1 - right) + top
    far_slot = 2 * (1 - right) + 1 - top
    for w in range(2):
        value = -mul_t(held[w, 0], mate[w, 0:side, :]) - mul_t(held[w, 3], mate[w, side:, :])
        put(2 * w, w, mate_slot, value)
    put(4, 0, cross_slot, -mul_t(held[0, 2], cross[0:side, :]) - mul_t(held[0, 1], cross[side:, :]))
    put(5, 0, far_slot, -mul_t(held[0, 2], far[0:side, :]) - mul_t(held[0, 3], far[side:, :]))
    for load in loads:
        load.wait()
    for w in range(2):
        value = diagonal[w] - mul_t(held[w, 0], own[w, 0:side, :]) - mul_t(held[w, 1], own[w, side:, :])
        put(2 * w + 1, w, 2 * right + top, value)
    for store in stores:
        store.wait()


def near_call(tiles, held, own, mate, cross, far):
    waves, side = tiles.shape[0], tiles.shape[1] // 4
    vmem = pl.BlockSpec(memory_space=pltpu.VMEM)
    return pl.pallas_call(
        functools.partial(near_kernel, side),
        name="near_columns",
        out_shape=jax.ShapeDtypeStruct((waves, 2 * side, 8 * side), jnp.float32),
        in_specs=[pl.BlockSpec(memory_space=pl.ANY)] + [vmem] * 5,
        out_specs=pl.BlockSpec(memory_space=pl.ANY),
        scratch_shapes=[
            pltpu.VMEM((waves, 2 * side, 2 * side), jnp.float32),
            pltpu.VMEM((3 * waves, 2 * side, 2 * side), jnp.float32),
            pltpu.SemaphoreType.DMA((4 * waves,)),
            pltpu.SemaphoreType.DMA((3 * waves,)),
        ],
        compiler_params=pltpu.CompilerParams(vmem_limit_bytes=32 << 20),
        cost_estimate=pl.CostEstimate(flops=12 * (2 * side) ** 3, bytes_accessed=1 << 20, transcendentals=0),
    )(tiles, held, own, mate, cross, far)


def last_kernel(side, before, held, cross_a, cross_b, far_a, far_b, out, buffer, sems):
    del before
    right, top = role()
    cross_slot = 2 * (1 - right) + top
    far_slot = 2 * (1 - right) + 1 - top
    stores = []
    for n, (slot, near, start, block) in enumerate(
        (
            (cross_slot, 1, 0, cross_a),
            (far_slot, 3, 0, far_a),
            (cross_slot, 1, side, cross_b),
            (far_slot, 3, side, far_b),
        )
    ):
        buffer[n] = -mul_t(held[1, 2], block[0:side, :]) - mul_t(held[1, near], block[side:, :])
        column = pl.multiple_of(slot * 2 * side + start, side)
        stores.append(pltpu.make_async_copy(buffer.at[n], out.at[1, :, pl.ds(column, side)], sems.at[n]))
        stores[-1].start()
    for store in stores:
        store.wait()


def last_call(before, held, *pieces):
    side = held.shape[2]
    vmem = pl.BlockSpec(memory_space=pltpu.VMEM)
    return pl.pallas_call(
        functools.partial(last_kernel, side),
        name="last_columns",
        out_shape=jax.ShapeDtypeStruct(before.shape, jnp.float32),
        in_specs=[pl.BlockSpec(memory_space=pl.ANY)] + [vmem] * 5,
        out_specs=pl.BlockSpec(memory_space=pl.ANY),
        scratch_shapes=[
            pltpu.VMEM((4, 2 * side, side), jnp.float32),
            pltpu.SemaphoreType.DMA((4,)),
        ],
        input_output_aliases={0: 0},
        compiler_params=pltpu.CompilerParams(vmem_limit_bytes=32 << 20),
        cost_estimate=pl.CostEstimate(flops=4 * (2 * side) ** 3, bytes_accessed=1 << 20, transcendentals=0),
    )(before, held, *pieces)


def body(children):
    tiles = children[:, 0, 0]
    waves, side = tiles.shape[0], tiles.shape[1] // 4
    pack = interfaces(tiles)
    whole, *parts = couplings(tiles)
    mate_pack = swapped(pack, "gy")
    cross_pack = swapped(pack, "gx")
    far_pack = swapped(cross_pack, "gy")
    mate = swapped(whole, "gy")
    previous = cross_pack
    cross = []
    far = []
    for part in parts:
        previous = swapped(after(part, previous), "gx")
        cross.append(previous)
        far.append(swapped(previous, "gy"))
    square = side * side
    matrix, sides = (waves, 5, side, side), (waves, 3, side, 2 * side)
    one, sides_one = whole_call(
        functools.partial(first_kernel, side), "eliminate_y", [matrix, sides], 20 * waves * square * side
    )(pack, mate_pack, whole)
    two, sides_two = whole_call(
        functools.partial(second_kernel, side), "eliminate_x", [matrix, sides], 20 * waves * square * side
    )(cross_pack, one, sides_one)
    (held,) = whole_call(
        functools.partial(third_kernel, side),
        "eliminate_far",
        [(waves, 4, side, 2 * side)],
        40 * waves * square * side,
    )(far_pack, one, sides_one, two, sides_two)
    near = near_call(tiles, held, whole, mate, cross[0], far[0])
    merged = last_call(near, held, cross[1], cross[2], far[1], far[2])
    return merged[:, None, None]


def solution(mesh):
    placed = (P("groups", "gx", "gy", None, None),)
    return jax.shard_map(
        body,
        mesh=mesh,
        in_specs=placed,
        out_specs=P("groups", "gx", "gy", None, None),
        check_vma=False,
    )
```

```python
import functools

import jax
import jax.numpy as jnp
from jax import lax
from jax.experimental import pallas as pl
from jax.experimental.pallas import tpu as pltpu
from jax.sharding import PartitionSpec as P

SUB = 8


def swapped(block, axis):
    count = lax.axis_size(axis)
    bit = count.bit_length() - 2
    route = []
    for low in range(count):
        high = low | 1 << bit
        if high != low and high < count:
            route += [(low, high), (high, low)]
    return lax.ppermute(block, axis, route)


def after(block, other):
    return lax.optimization_barrier((block, other))[0]


def role():
    right = (lax.axis_index("gx") >= lax.axis_size("gx") // 2).astype(jnp.int32)
    top = (lax.axis_index("gy") >= lax.axis_size("gy") // 2).astype(jnp.int32)
    return right, top


def mul(a, b):
    return lax.dot_general(
        a, b, (((1,), (0,)), ((), ())), precision=lax.Precision.HIGHEST, preferred_element_type=jnp.float32
    )


def mul_t(a, b):
    return lax.dot_general(
        a, b, (((0,), (0,)), ((), ())), precision=lax.Precision.HIGHEST, preferred_element_type=jnp.float32
    )


def work(microseconds):
    return int(microseconds * 1e9)


def tree(terms):
    while len(terms) > 1:
        terms = [terms[i] + terms[i + 1] for i in range(0, len(terms) - 1, 2)] + terms[len(terms) & ~1 :]
    return terms[0]


def inverses(matrices):
    size = matrices[0].shape[0]
    panels = size // SUB
    many = len(matrices)
    lane = lax.broadcasted_iota(jnp.int32, (SUB, size), 1)
    sub = lax.broadcasted_iota(jnp.int32, (SUB, size), 0)

    def full(v):
        return jnp.broadcast_to(v, (SUB, size))

    state = [[m[SUB * i : SUB * i + SUB, :] for i in range(panels)] for m in matrices]
    lower = [[] for _ in matrices]
    scaled = [[] for _ in matrices]
    for p in range(panels):
        first = SUB * p
        inside = (lane >= first) & (lane < first + SUB)
        unit = jnp.where(lane - first == sub, 1.0, 0.0)
        done = lane < first + SUB
        blocks = [[full(state[w][p][:, first + j : first + j + 1]) for j in range(SUB)] for w in range(many)]
        raw = [state[w][p] for w in range(many)]
        panel = [jnp.where(inside, unit, raw[w]) for w in range(many)]
        for w in range(many):
            lower[w].append(jnp.where(done, panel[w], 0.0))
        for k in range(SUB):
            at_row = sub == k
            for w in range(many):
                block = blocks[w]
                inverse = 1.0 / full(block[k][k : k + 1])
                factor = jnp.where(at_row, -1.0, block[k])

                def step(x):
                    return jnp.where(at_row, 0.0, x) - (factor * full(x[k : k + 1])) * inverse

                for j in range(k + 1, SUB):
                    block[j] = step(block[j])
                panel[w] = step(panel[w])
        for w in range(many):
            gained, rows = panel[w], state[w]
            scaled[w].append(jnp.where(done, gained, 0.0))
            if p + 2 < panels:
                change = mul_t(raw[w], gained)
                for i in range(p + 2, panels):
                    rows[i] = jnp.where(inside, 0.0, rows[i]) - change[SUB * i : SUB * i + SUB]
            if p + 1 < panels:
                row = rows[p + 1]
                terms = [full(row[:, first + l : first + l + 1]) * full(gained[l : l + 1]) for l in range(SUB)]
                rows[p + 1] = jnp.where(inside, 0.0, row) - tree(terms)
    return [mul_t(jnp.concatenate(lower[w], 0), jnp.concatenate(scaled[w], 0)) for w in range(many)]


def square_masks(side):
    row = lax.broadcasted_iota(jnp.int32, (side, side), 0)
    col = lax.broadcasted_iota(jnp.int32, (side, side), 1)
    return row > col, row == col


def pack_yy(square):
    below, diag = square_masks(square.shape[0])
    return jnp.where(below | diag, square, square.T)


def pack_xx(square, line):
    below, diag = square_masks(square.shape[0])
    return jnp.where(diag, jnp.broadcast_to(line, square.shape), jnp.where(below, square.T, square))


def interface_kernel(side, tiles, pack, own_yy, own_xx, sems):
    right, top = role()
    side_y = 3 - top
    side_x = 1 - right
    waves = pack.shape[0]

    def piece(w, row_side, col_side):
        rows = pl.ds(pl.multiple_of(row_side * side, side), side)
        cols = pl.ds(pl.multiple_of(col_side * side, side), side)
        return tiles.at[w, rows, cols]

    copies = []
    for w in range(waves):
        copies += [
            pltpu.make_async_copy(piece(w, side_y, side_y), own_yy.at[w], sems.at[3 * w]),
            pltpu.make_async_copy(piece(w, side_x, side_x), own_xx.at[w], sems.at[3 * w + 1]),
            pltpu.make_async_copy(piece(w, side_y, side_x), pack.at[w, pl.ds(side, side), :], sems.at[3 * w + 2]),
        ]
    for copy in copies:
        copy.start()
    below, diag = square_masks(side)
    for w in range(waves):
        copies[3 * w].wait()
        copies[3 * w + 1].wait()
        xx = own_xx[w]
        pack[w, 0:side, :] = jnp.where(below | diag, own_yy[w], xx)
        line = jnp.sum(jnp.where(diag, xx, 0.0), 0, keepdims=True)
        pack[w, 2 * side :, :] = jnp.broadcast_to(line, (SUB, side))
    for w in range(waves):
        copies[3 * w + 2].wait()


def interfaces(tiles):
    waves, side = tiles.shape[0], tiles.shape[1] // 4
    return pl.pallas_call(
        functools.partial(interface_kernel, side),
        name="interfaces",
        out_shape=jax.ShapeDtypeStruct((waves, 2 * side + SUB, side), jnp.float32),
        in_specs=[pl.BlockSpec(memory_space=pl.ANY)],
        out_specs=pl.BlockSpec(memory_space=pltpu.VMEM),
        scratch_shapes=[
            pltpu.VMEM((waves, side, side), jnp.float32),
            pltpu.VMEM((waves, side, side), jnp.float32),
            pltpu.SemaphoreType.DMA((3 * waves,)),
        ],
        cost_estimate=pl.CostEstimate(flops=work(1.5), bytes_accessed=5 * waves * side * side * 4, transcendentals=0),
    )(tiles)


def coupling_kernel(side, tiles, whole, first, second, third, sems):
    right, top = role()
    rows_of = (3 - top, 1 - right)
    cols_of = (right, 2 + top)
    copies = []
    for w in range(2):
        for i in range(2):
            rows = pl.ds(pl.multiple_of(rows_of[i] * side, side), side)
            here = pl.ds(i * side, side)
            for j in range(2):
                cols = pl.ds(pl.multiple_of(cols_of[j] * side, side), side)
                source = tiles.at[w, rows, cols]
                there = pl.ds(j * side, side)
                n = len(copies)
                copies.append(pltpu.make_async_copy(source, whole.at[w, here, there], sems.at[n]))
                if w == 0:
                    target = first.at[here, there]
                else:
                    target = (second, third)[j].at[here, :]
                copies.append(pltpu.make_async_copy(source, target, sems.at[n + 1]))
    for copy in copies:
        copy.start()
    for copy in copies:
        copy.wait()


def couplings(tiles):
    waves, side = tiles.shape[0], tiles.shape[1] // 4
    shapes = [(waves, 2 * side, 2 * side), (2 * side, 2 * side), (2 * side, side), (2 * side, side)]
    return pl.pallas_call(
        functools.partial(coupling_kernel, side),
        name="couplings",
        out_shape=[jax.ShapeDtypeStruct(s, jnp.float32) for s in shapes],
        in_specs=[pl.BlockSpec(memory_space=pl.ANY)],
        out_specs=[pl.BlockSpec(memory_space=pltpu.VMEM)] * 4,
        scratch_shapes=[pltpu.SemaphoreType.DMA((8 * waves,))],
        cost_estimate=pl.CostEstimate(flops=work(2), bytes_accessed=16 * waves * side * side * 4, transcendentals=0),
    )(tiles)


def first_kernel(side, own, mate, coupling, solved, rest):
    waves = own.shape[0]
    inverse = inverses([pack_yy(own[w, 0:side, :] + mate[w, 0:side, :]) for w in range(waves)])
    for w in range(waves):
        across = jnp.concatenate([own[w, side : 2 * side, :], mate[w, side : 2 * side, :]], 1)
        gains = mul(inverse[w], jnp.concatenate([across, coupling[w, 0:side, :]], 1))
        solved[w] = gains
        change = mul_t(across, gains)
        lines = own[w, 2 * side : 2 * side + 1, :], mate[w, 2 * side : 2 * side + 1, :]
        rest[w, 0:side, 0:side] = pack_xx(own[w, 0:side, :], lines[0]) - change[0:side, 0:side]
        rest[w, 0:side, side : 2 * side] = -change[0:side, side : 2 * side]
        rest[w, 0:side, 2 * side :] = coupling[w, side:, :] - change[0:side, 2 * side :]
        rest[w, side:, 0:side] = -change[side:, 0:side]
        rest[w, side:, side : 2 * side] = pack_xx(mate[w, 0:side, :], lines[1]) - change[side:, side : 2 * side]
        rest[w, side:, 2 * side :] = -change[side:, 2 * side :]


def second_kernel(side, pack, solved_y, rest, solved, left):
    waves = pack.shape[0]
    inverse = inverses(
        [
            rest[w, 0:side, 0:side] + pack_xx(pack[w, 0:side, :], pack[w, 2 * side : 2 * side + 1, :])
            for w in range(waves)
        ]
    )
    for w in range(waves):
        vx = pack[w, side : 2 * side, :]
        gains = mul(inverse[w], jnp.concatenate([vx.T, rest[w, 0:side, side:]], 1))
        solved[w] = gains
        column = jnp.concatenate([vx, rest[w, side:, 0:side], solved_y[w, :, 0:side]], 0)
        change = mul(column, gains)
        left[w, 0:side, 0:side] = pack_yy(pack[w, 0:side, :]) - change[0:side, 0:side]
        left[w, 0:side, side:] = -change[0:side, side:]
        left[w, side:, 0:side] = -change[side:, 0:side]
        left[w, side : 2 * side, side:] = rest[w, side:, side:] - change[side : 2 * side, side:]
        left[w, 2 * side :, side:] = solved_y[w, :, side:] - change[2 * side :, side:]


def third_kernel(side, pack, solved_x, left, solved, last):
    waves = pack.shape[0]
    inverse = inverses([left[w, 0:side, 0:side] + pack_yy(pack[w, 0:side, :]) for w in range(waves)])
    for w in range(waves):
        vu = pack[w, side : 2 * side, :]
        row = jnp.concatenate([left[w, 0:side, side : 2 * side] + vu, left[w, 0:side, 2 * side :]], 1)
        gains = mul(inverse[w], row)
        solved[w] = gains
        column = jnp.concatenate(
            [left[w, side : 2 * side, 0:side] + vu.T, left[w, 2 * side :, 0:side], solved_x[w, :, 0:side]], 0
        )
        change = mul(column, gains)
        uu = pack_xx(pack[w, 0:side, :], pack[w, 2 * side : 2 * side + 1, :])
        last[w, 0:side, 0:side] = left[w, side : 2 * side, side : 2 * side] + uu - change[0:side, 0:side]
        last[w, 0:side, side:] = left[w, side : 2 * side, 2 * side :] - change[0:side, side:]
        last[w, side : 2 * side, :] = left[w, 2 * side :, side:] - change[side : 2 * side, :]
        last[w, 2 * side :, :] = solved_x[w, :, side:] - change[2 * side :, :]


def fourth_kernel(side, solved_v, last, held):
    waves = last.shape[0]
    inverse = inverses([last[w, 0:side, 0:side] for w in range(waves)])
    for w in range(waves):
        held_u = mul(inverse[w], last[w, 0:side, side:])
        change = mul(jnp.concatenate([last[w, side:, 0:side], solved_v[w, :, 0:side]], 0), held_u)
        held[w, 0] = last[w, side : 2 * side, side:] - change[0:side]
        held[w, 1] = last[w, 2 * side :, side:] - change[side : 2 * side]
        held[w, 2] = solved_v[w, :, side:] - change[2 * side :]
        held[w, 3] = held_u


def whole_call(kernel, name, shapes, flops):
    return lambda *args: pl.pallas_call(
        kernel,
        name=name,
        out_shape=[jax.ShapeDtypeStruct(s, jnp.float32) for s in shapes],
        in_specs=[pl.BlockSpec(memory_space=pltpu.VMEM)] * len(args),
        out_specs=[pl.BlockSpec(memory_space=pltpu.VMEM)] * len(shapes),
        compiler_params=pltpu.CompilerParams(vmem_limit_bytes=32 << 20),
        cost_estimate=pl.CostEstimate(flops=flops, bytes_accessed=1 << 20, transcendentals=0),
    )(*args)


def near_kernel(side, tiles, held, own, mate, cross, far, out, diagonal, buffer, load_sems, sems):
    right, top = role()
    sides = (right, 2 + top)
    loads = []
    for w in range(2):
        for i in range(2):
            rows = pl.ds(pl.multiple_of(sides[i] * side, side), side)
            for j in range(2):
                cols = pl.ds(pl.multiple_of(sides[j] * side, side), side)
                loads.append(
                    pltpu.make_async_copy(
                        tiles.at[w, rows, cols],
                        diagonal.at[w, pl.ds(i * side, side), pl.ds(j * side, side)],
                        load_sems.at[len(loads)],
                    )
                )
                loads[-1].start()
    stores = []

    def put(n, w, slot, value):
        buffer[n] = value
        column = pl.multiple_of(slot * 2 * side, 2 * side)
        stores.append(pltpu.make_async_copy(buffer.at[n], out.at[w, :, pl.ds(column, 2 * side)], sems.at[n]))
        stores[-1].start()

    mate_slot = 2 * right + 1 - top
    cross_slot = 2 * (1 - right) + top
    far_slot = 2 * (1 - right) + 1 - top
    for w in range(2):
        value = -mul_t(held[w, 0], mate[w, 0:side, :]) - mul_t(held[w, 3], mate[w, side:, :])
        put(2 * w, w, mate_slot, value)
    put(4, 0, cross_slot, -mul_t(held[0, 2], cross[0:side, :]) - mul_t(held[0, 1], cross[side:, :]))
    put(5, 0, far_slot, -mul_t(held[0, 2], far[0:side, :]) - mul_t(held[0, 3], far[side:, :]))
    for load in loads:
        load.wait()
    for w in range(2):
        value = diagonal[w] - mul_t(held[w, 0], own[w, 0:side, :]) - mul_t(held[w, 1], own[w, side:, :])
        put(2 * w + 1, w, 2 * right + top, value)
    for store in stores:
        store.wait()


def near_call(tiles, held, own, mate, cross, far):
    waves, side = tiles.shape[0], tiles.shape[1] // 4
    vmem = pl.BlockSpec(memory_space=pltpu.VMEM)
    return pl.pallas_call(
        functools.partial(near_kernel, side),
        name="near_columns",
        out_shape=jax.ShapeDtypeStruct((waves, 2 * side, 8 * side), jnp.float32),
        in_specs=[pl.BlockSpec(memory_space=pl.ANY)] + [vmem] * 5,
        out_specs=pl.BlockSpec(memory_space=pl.ANY),
        scratch_shapes=[
            pltpu.VMEM((waves, 2 * side, 2 * side), jnp.float32),
            pltpu.VMEM((3 * waves, 2 * side, 2 * side), jnp.float32),
            pltpu.SemaphoreType.DMA((4 * waves,)),
            pltpu.SemaphoreType.DMA((3 * waves,)),
        ],
        compiler_params=pltpu.CompilerParams(vmem_limit_bytes=32 << 20),
        cost_estimate=pl.CostEstimate(flops=work(4), bytes_accessed=1 << 20, transcendentals=0),
    )(tiles, held, own, mate, cross, far)


def last_kernel(side, before, held, cross_a, cross_b, far_a, far_b, out, buffer, sems):
    del before
    right, top = role()
    cross_slot = 2 * (1 - right) + top
    far_slot = 2 * (1 - right) + 1 - top
    stores = []
    for n, (slot, near, start, block) in enumerate(
        (
            (cross_slot, 1, 0, cross_a),
            (far_slot, 3, 0, far_a),
            (cross_slot, 1, side, cross_b),
            (far_slot, 3, side, far_b),
        )
    ):
        buffer[n] = -mul_t(held[1, 2], block[0:side, :]) - mul_t(held[1, near], block[side:, :])
        column = pl.multiple_of(slot * 2 * side + start, side)
        stores.append(pltpu.make_async_copy(buffer.at[n], out.at[1, :, pl.ds(column, side)], sems.at[n]))
        stores[-1].start()
    for store in stores:
        store.wait()


def last_call(before, held, *pieces):
    side = held.shape[2]
    vmem = pl.BlockSpec(memory_space=pltpu.VMEM)
    return pl.pallas_call(
        functools.partial(last_kernel, side),
        name="last_columns",
        out_shape=jax.ShapeDtypeStruct(before.shape, jnp.float32),
        in_specs=[pl.BlockSpec(memory_space=pl.ANY)] + [vmem] * 5,
        out_specs=pl.BlockSpec(memory_space=pl.ANY),
        scratch_shapes=[
            pltpu.VMEM((4, 2 * side, side), jnp.float32),
            pltpu.SemaphoreType.DMA((4,)),
        ],
        input_output_aliases={0: 0},
        compiler_params=pltpu.CompilerParams(vmem_limit_bytes=32 << 20),
        cost_estimate=pl.CostEstimate(flops=work(2), bytes_accessed=1 << 20, transcendentals=0),
    )(before, held, *pieces)


def body(children):
    tiles = children[:, 0, 0]
    waves, side = tiles.shape[0], tiles.shape[1] // 4
    pack = interfaces(tiles)
    whole, *parts = couplings(tiles)
    mate_pack = swapped(pack, "gy")
    cross_pack = swapped(pack, "gx")
    mate = swapped(whole, "gy")

    def eliminate(kernel, name, shapes, time):
        return whole_call(functools.partial(kernel, side), name, [(waves, *shape) for shape in shapes], work(time))

    full = 4 * side
    solved_y, rest = eliminate(first_kernel, "eliminate_y", [(side, full), (2 * side, full)], 7)(
        pack, mate_pack, whole
    )
    cross_0 = swapped(after(parts[0], (cross_pack, solved_y)), "gx")
    far_pack = swapped(cross_pack, "gy")
    solved_x, left = eliminate(second_kernel, "eliminate_x", [(side, full), (3 * side, full)], 7)(
        cross_pack, solved_y, rest
    )
    cross_1 = swapped(after(parts[1], (cross_0, solved_x)), "gx")
    solved_v, last = eliminate(third_kernel, "eliminate_v", [(side, 3 * side), (3 * side, 3 * side)], 7)(
        far_pack, solved_x, left
    )
    far_0 = swapped(cross_0, "gy")
    cross_2 = swapped(after(parts[2], (cross_1, solved_v)), "gx")
    far_1 = swapped(cross_1, "gy")
    (held,) = eliminate(fourth_kernel, "eliminate_u", [(4, side, 2 * side)], 7)(solved_v, last)
    far_2 = swapped(cross_2, "gy")
    cross, far = (cross_0, cross_1, cross_2), (far_0, far_1, far_2)
    near = near_call(tiles, held, whole, mate, cross[0], far[0])
    merged = last_call(near, held, cross[1], cross[2], far[1], far[2])
    return merged[:, None, None]


def solution(mesh):
    placed = (P("groups", "gx", "gy", None, None),)
    return jax.shard_map(
        body,
        mesh=mesh,
        in_specs=placed,
        out_specs=P("groups", "gx", "gy", None, None),
        check_vma=False,
    )
```

```python
import functools

import jax
import jax.numpy as jnp
from jax import lax
from jax.experimental import pallas as pl
from jax.experimental.pallas import tpu as pltpu
from jax.sharding import PartitionSpec as P

SUB = 8


def swapped(block, axis):
    count = lax.axis_size(axis)
    bit = count.bit_length() - 2
    route = []
    for low in range(count):
        high = low | 1 << bit
        if high != low and high < count:
            route += [(low, high), (high, low)]
    return lax.ppermute(block, axis, route)


def after(block, other):
    return lax.optimization_barrier((block, other))[0]


def role():
    right = (lax.axis_index("gx") >= lax.axis_size("gx") // 2).astype(jnp.int32)
    top = (lax.axis_index("gy") >= lax.axis_size("gy") // 2).astype(jnp.int32)
    return right, top


def mul(a, b):
    return lax.dot_general(
        a, b, (((1,), (0,)), ((), ())), precision=lax.Precision.HIGHEST, preferred_element_type=jnp.float32
    )


def mul_t(a, b):
    return lax.dot_general(
        a, b, (((0,), (0,)), ((), ())), precision=lax.Precision.HIGHEST, preferred_element_type=jnp.float32
    )


def work(microseconds):
    return int(microseconds * 1e9)


def tree(terms):
    while len(terms) > 1:
        terms = [terms[i] + terms[i + 1] for i in range(0, len(terms) - 1, 2)] + terms[len(terms) & ~1 :]
    return terms[0]


def inverses(matrices):
    size = matrices[0].shape[0]
    panels = size // SUB
    many = len(matrices)
    lane = lax.broadcasted_iota(jnp.int32, (SUB, size), 1)
    sub = lax.broadcasted_iota(jnp.int32, (SUB, size), 0)

    def full(v):
        return jnp.broadcast_to(v, (SUB, size))

    state = [[m[SUB * i : SUB * i + SUB, :] for i in range(panels)] for m in matrices]
    lower = [[] for _ in matrices]
    scaled = [[] for _ in matrices]
    for p in range(panels):
        first = SUB * p
        inside = (lane >= first) & (lane < first + SUB)
        unit = jnp.where(lane - first == sub, 1.0, 0.0)
        done = lane < first + SUB
        blocks = [[full(state[w][p][:, first + j : first + j + 1]) for j in range(SUB)] for w in range(many)]
        panel = [jnp.where(inside, unit, state[w][p]) for w in range(many)]
        for w in range(many):
            lower[w].append(jnp.where(done, panel[w], 0.0))
        for k in range(SUB):
            at_row = sub == k
            for w in range(many):
                block = blocks[w]
                inverse = 1.0 / full(block[k][k : k + 1])
                factor = jnp.where(at_row, -1.0, block[k])

                def step(x):
                    return jnp.where(at_row, 0.0, x) - (factor * full(x[k : k + 1])) * inverse

                for j in range(k + 1, SUB):
                    block[j] = step(block[j])
                panel[w] = step(panel[w])
        for w in range(many):
            gained, rows = panel[w], state[w]
            scaled[w].append(jnp.where(done, gained, 0.0))
            if p + 2 < panels:
                below = jnp.concatenate(rows[p + 2 :], 0)
                within = jnp.concatenate([inside] * (panels - p - 2), 0)
                empty = jnp.zeros((SUB, size), jnp.float32)
                placed = jnp.concatenate([gained if i == p else empty for i in range(panels)], 0)
                change = mul(jnp.where(within, below, 0.0), placed)
                for i in range(p + 2, panels):
                    at = SUB * (i - p - 2)
                    rows[i] = jnp.where(inside, 0.0, rows[i]) - change[at : at + SUB]
            if p + 1 < panels:
                row = rows[p + 1]
                terms = [full(row[:, first + l : first + l + 1]) * full(gained[l : l + 1]) for l in range(SUB)]
                rows[p + 1] = jnp.where(inside, 0.0, row) - tree(terms)
    return [mul_t(jnp.concatenate(lower[w], 0), jnp.concatenate(scaled[w], 0)) for w in range(many)]


def square_masks(side):
    row = lax.broadcasted_iota(jnp.int32, (side, side), 0)
    col = lax.broadcasted_iota(jnp.int32, (side, side), 1)
    return row > col, row == col


def pack_yy(square):
    below, diag = square_masks(square.shape[0])
    return jnp.where(below | diag, square, square.T)


def pack_xx(square, line):
    below, diag = square_masks(square.shape[0])
    return jnp.where(diag, jnp.broadcast_to(line, square.shape), jnp.where(below, square.T, square))


def block_of(tiles, side, w, row_side, col_side):
    rows = pl.ds(pl.multiple_of(row_side * side, side), side)
    cols = pl.ds(pl.multiple_of(col_side * side, side), side)
    return tiles.at[w, rows, cols]


def height(side):
    return 2 * side + SUB


def pack_kernel(side, units, tiles, own, sent, own_yy, own_xx, own_yx, sems, unit_sems):
    right, top = role()
    inner, outer = (3 - top, 1 - right), (right, 2 + top)
    waves = own_yy.shape[0]
    tall = height(side)
    copies = []
    for w in range(waves):
        for n, (i, j, target) in enumerate(((0, 0, own_yy), (1, 1, own_xx), (0, 1, own_yx))):
            source = block_of(tiles, side, w, inner[i], inner[j])
            copies.append(pltpu.make_async_copy(source, target.at[w], sems.at[3 * w + n]))
            copies[-1].start()
    others = load_units(tiles, side, inner, outer, units, sent, waves * tall, unit_sems, 0)
    below, diag = square_masks(side)
    for w in range(waves):
        for copy in copies[3 * w : 3 * w + 3]:
            copy.wait()
        xx = own_xx[w]
        square = jnp.where(below | diag, own_yy[w], xx)
        line = jnp.broadcast_to(jnp.sum(jnp.where(diag, xx, 0.0), 0, keepdims=True), (SUB, side))
        for target in (own, sent):
            target[w * tall : w * tall + side, :] = square
            target[w * tall + side : w * tall + 2 * side, :] = own_yx[w]
            target[w * tall + 2 * side : (w + 1) * tall, :] = line
    for copy in others:
        copy.wait()


def load_units(tiles, side, inner, outer, units, target, base, sems, first):
    copies = []
    for n, unit in enumerate(units):
        w, j = divmod(unit, 2)
        for i in range(2):
            place = target.at[pl.ds(base + (2 * n + i) * side, side), :]
            source = block_of(tiles, side, w, inner[i], outer[j])
            copies.append(pltpu.make_async_copy(source, place, sems.at[first + len(copies)]))
            copies[-1].start()
    return copies


def packed(tiles, units):
    waves, side = tiles.shape[0], tiles.shape[1] // 4
    square = pltpu.VMEM((waves, side, side), jnp.float32)
    rows = waves * height(side)
    return pl.pallas_call(
        functools.partial(pack_kernel, side, units),
        name="pack",
        out_shape=[
            jax.ShapeDtypeStruct((rows, side), jnp.float32),
            jax.ShapeDtypeStruct((rows + len(units) * 2 * side, side), jnp.float32),
        ],
        in_specs=[pl.BlockSpec(memory_space=pl.ANY)],
        out_specs=[pl.BlockSpec(memory_space=pltpu.VMEM)] * 2,
        scratch_shapes=[
            square,
            square,
            square,
            pltpu.SemaphoreType.DMA((3 * waves,)),
            pltpu.SemaphoreType.DMA((2 * len(units),)),
        ],
        cost_estimate=pl.CostEstimate(flops=work(1.5), bytes_accessed=1 << 20, transcendentals=0),
    )(tiles)


def coupling_kernel(side, groups, tiles, *refs):
    targets, sems = refs[:-1], refs[-1]
    right, top = role()
    inner, outer = (3 - top, 1 - right), (right, 2 + top)
    copies = []
    for units, target in zip(groups, targets):
        copies += load_units(tiles, side, inner, outer, units, target, 0, sems, len(copies))
    for copy in copies:
        copy.wait()


def couplings(tiles, groups):
    side = tiles.shape[1] // 4
    count = sum(len(units) for units in groups)
    return pl.pallas_call(
        functools.partial(coupling_kernel, side, groups),
        name="couplings",
        out_shape=[jax.ShapeDtypeStruct((len(units) * 2 * side, side), jnp.float32) for units in groups],
        in_specs=[pl.BlockSpec(memory_space=pl.ANY)],
        out_specs=[pl.BlockSpec(memory_space=pltpu.VMEM)] * len(groups),
        scratch_shapes=[pltpu.SemaphoreType.DMA((2 * count,))],
        cost_estimate=pl.CostEstimate(flops=work(2), bytes_accessed=2 << 20, transcendentals=0),
    )(tiles)


def parts_of(pack, side, w):
    base = w * height(side)
    return pack[base : base + side, :], pack[base + side : base + 2 * side, :], pack[base + 2 * side : base + 2 * side + 1, :]


def load_blocks(tiles, side, row_sides, col_sides, target, sems):
    copies = []
    for w in range(target.shape[0]):
        for i in range(2):
            for j in range(2):
                place = target.at[w, pl.ds(i * side, side), pl.ds(j * side, side)]
                source = block_of(tiles, side, w, row_sides[i], col_sides[j])
                copies.append(pltpu.make_async_copy(source, place, sems.at[len(copies)]))
                copies[-1].start()
    return copies


def first_kernel(side, own, mate, tiles, solved, rest, coupling, sems):
    waves = solved.shape[0]
    right, top = role()
    loads = load_blocks(tiles, side, (3 - top, 1 - right), (right, 2 + top), coupling, sems)
    ours = [parts_of(own, side, w) for w in range(waves)]
    theirs = [parts_of(mate, side, w) for w in range(waves)]
    inverse = inverses([pack_yy(ours[w][0] + theirs[w][0]) for w in range(waves)])
    for load in loads:
        load.wait()
    for w in range(waves):
        across = jnp.concatenate([ours[w][1], theirs[w][1]], 1)
        gains = mul(inverse[w], jnp.concatenate([across, coupling[w, 0:side, :]], 1))
        solved[w] = gains
        change = mul_t(across, gains)
        rest[w, 0:side, 0:side] = pack_xx(ours[w][0], ours[w][2]) - change[0:side, 0:side]
        rest[w, 0:side, side : 2 * side] = -change[0:side, side : 2 * side]
        rest[w, 0:side, 2 * side :] = coupling[w, side:, :] - change[0:side, 2 * side :]
        rest[w, side:, 0:side] = -change[side:, 0:side]
        rest[w, side:, side : 2 * side] = pack_xx(theirs[w][0], theirs[w][2]) - change[side:, side : 2 * side]
        rest[w, side:, 2 * side :] = -change[side:, 2 * side :]


def second_kernel(side, pack, solved_y, rest, solved, left):
    waves = solved.shape[0]
    parts = [parts_of(pack, side, w) for w in range(waves)]
    inverse = inverses([rest[w, 0:side, 0:side] + pack_xx(parts[w][0], parts[w][2]) for w in range(waves)])
    for w in range(waves):
        vx = parts[w][1]
        gains = mul(inverse[w], jnp.concatenate([vx.T, rest[w, 0:side, side:]], 1))
        solved[w] = gains
        column = jnp.concatenate([vx, rest[w, side:, 0:side], solved_y[w, :, 0:side]], 0)
        change = mul(column, gains)
        left[w, 0:side, 0:side] = pack_yy(parts[w][0]) - change[0:side, 0:side]
        left[w, 0:side, side:] = -change[0:side, side:]
        left[w, side:, 0:side] = -change[side:, 0:side]
        left[w, side : 2 * side, side:] = rest[w, side:, side:] - change[side : 2 * side, side:]
        left[w, 2 * side :, side:] = solved_y[w, :, side:] - change[2 * side :, side:]


def third_kernel(side, pack, solved_x, left, solved, last):
    waves = solved.shape[0]
    parts = [parts_of(pack, side, w) for w in range(waves)]
    inverse = inverses([left[w, 0:side, 0:side] + pack_yy(parts[w][0]) for w in range(waves)])
    for w in range(waves):
        vu = parts[w][1]
        row = jnp.concatenate([left[w, 0:side, side : 2 * side] + vu, left[w, 0:side, 2 * side :]], 1)
        gains = mul(inverse[w], row)
        solved[w] = gains
        column = jnp.concatenate(
            [left[w, side : 2 * side, 0:side] + vu.T, left[w, 2 * side :, 0:side], solved_x[w, :, 0:side]], 0
        )
        change = mul(column, gains)
        uu = pack_xx(parts[w][0], parts[w][2])
        last[w, 0:side, 0:side] = left[w, side : 2 * side, side : 2 * side] + uu - change[0:side, 0:side]
        last[w, 0:side, side:] = left[w, side : 2 * side, 2 * side :] - change[0:side, side:]
        last[w, side : 2 * side, :] = left[w, 2 * side :, side:] - change[side : 2 * side, :]
        last[w, 2 * side :, :] = solved_x[w, :, side:] - change[2 * side :, :]


def fourth_kernel(side, solved_v, last, held):
    waves = last.shape[0]
    inverse = inverses([last[w, 0:side, 0:side] for w in range(waves)])
    for w in range(waves):
        held_u = mul(inverse[w], last[w, 0:side, side:])
        change = mul(jnp.concatenate([last[w, side:, 0:side], solved_v[w, :, 0:side]], 0), held_u)
        held[w, 0] = last[w, side : 2 * side, side:] - change[0:side]
        held[w, 1] = last[w, 2 * side :, side:] - change[side : 2 * side]
        held[w, 2] = solved_v[w, :, side:] - change[2 * side :]
        held[w, 3] = held_u


def whole_call(kernel, name, shapes, time, tiles=None, scratch=()):
    vmem = pl.BlockSpec(memory_space=pltpu.VMEM)

    def call(*args):
        specs = [vmem] * len(args)
        if tiles is not None:
            args = (*args, tiles)
            specs.append(pl.BlockSpec(memory_space=pl.ANY))
        return pl.pallas_call(
            kernel,
            name=name,
            out_shape=[jax.ShapeDtypeStruct(s, jnp.float32) for s in shapes],
            in_specs=specs,
            out_specs=[vmem] * len(shapes),
            scratch_shapes=list(scratch),
            compiler_params=pltpu.CompilerParams(vmem_limit_bytes=32 << 20),
            cost_estimate=pl.CostEstimate(flops=work(time), bytes_accessed=1 << 20, transcendentals=0),
        )(*args)

    return call


def split(x):
    high = x.astype(jnp.bfloat16)
    return high, (x - high.astype(jnp.float32)).astype(jnp.bfloat16)


def mul_split(a, b):
    dims = (((0,), (0,)), ((), ()))
    terms = [(a[0], b[0]), (a[0], b[1]), (a[1], b[0])]
    return sum(lax.dot_general(x, y, dims, preferred_element_type=jnp.float32) for x, y in terms)


MATE, CROSS, FAR = (0, 3), (2, 1), (2, 3)


def columns_kernel(side, groups, with_own, *refs):
    count = len(groups)
    if with_own:
        tiles, held, *arrays = refs[: 2 + count]
        out, coupling, diagonal, load_sems, buffer, sems = refs[2 + count :]
    else:
        _, held, *arrays = refs[: 2 + count]
        out, buffer, sems = refs[2 + count :]
    right, top = role()
    slots = {MATE: 2 * right + 1 - top, CROSS: 2 * (1 - right) + top, FAR: 2 * (1 - right) + 1 - top}
    waves = held.shape[0]
    inner, outer = (3 - top, 1 - right), (right, 2 + top)
    if with_own:
        loads = load_blocks(tiles, side, inner, outer, coupling, load_sems.at[0])
        loads += load_blocks(tiles, side, outer, outer, diagonal, load_sems.at[1])
    parts = {}

    def part(w, i):
        if (w, i) not in parts:
            parts[w, i] = split(held[w, i])
        return parts[w, i]

    def product(w, box, block):
        total = 0.0
        for n, i in enumerate(box):
            total += mul_split(part(w, i), split(block[n * side : (n + 1) * side]))
        return total

    stores = []

    def put(w, slot, j, value):
        n = len(stores)
        width = value.shape[1]
        buffer[n, :, 0:width] = value
        column = pl.multiple_of(slot * 2 * side + j * side, side)
        target = out.at[w, :, pl.ds(column, width)]
        stores.append(pltpu.make_async_copy(buffer.at[n, :, pl.ds(0, width)], target, sems.at[n]))
        stores[-1].start()

    for (box, units, base), array in zip(groups, arrays):
        n = 0
        while n < len(units):
            w, j = divmod(units[n], 2)
            pair = j == 0 and n + 1 < len(units) and units[n + 1] == units[n] + 1
            rows = [array[base + 2 * side * m : base + 2 * side * (m + 1), :] for m in range(n, n + 1 + pair)]
            block = jnp.concatenate(rows, 1)
            put(w, slots[box], j, -product(w, box, block))
            n += 2 if pair else 1
    if with_own:
        for load in loads:
            load.wait()
        for w in range(waves):
            put(w, 2 * right + top, 0, diagonal[w] - product(w, (0, 1), coupling[w]))
    for store in stores:
        store.wait()


def columns_call(name, time, source, held, pieces, with_own):
    waves, side = held.shape[0], held.shape[2]
    groups = tuple((box, units, base) for box, units, _, base in pieces)
    vmem, anywhere = pl.BlockSpec(memory_space=pltpu.VMEM), pl.BlockSpec(memory_space=pl.ANY)
    square = pltpu.VMEM((waves, 2 * side, 2 * side), jnp.float32)
    most = sum(len(units) for _, units, _, _ in pieces) + waves
    scratch = [pltpu.VMEM((most, 2 * side, 2 * side), jnp.float32), pltpu.SemaphoreType.DMA((most,))]
    if with_own:
        scratch = [square, square, pltpu.SemaphoreType.DMA((2, 4 * waves))] + scratch
    return pl.pallas_call(
        functools.partial(columns_kernel, side, groups, with_own),
        name=name,
        out_shape=jax.ShapeDtypeStruct((waves, 2 * side, 8 * side), jnp.float32),
        in_specs=[anywhere] + [vmem] * (1 + len(pieces)),
        out_specs=anywhere,
        scratch_shapes=scratch,
        input_output_aliases={} if with_own else {0: 0},
        compiler_params=pltpu.CompilerParams(vmem_limit_bytes=32 << 20),
        cost_estimate=pl.CostEstimate(flops=work(time), bytes_accessed=1 << 20, transcendentals=0),
    )(source, held, *(array for _, _, array, _ in pieces))


def body(children):
    tiles = children[:, 0, 0]
    waves, side = tiles.shape[0], tiles.shape[1] // 4
    units = tuple(range(2 * waves))
    first, second = units[:1], units[1:]
    base = waves * height(side)
    own, sent = packed(tiles, first)
    whole, part = couplings(tiles, (units, second))
    cross_0 = swapped(sent, "gx")
    mate_pack = swapped(own, "gy")
    mate = swapped(after(whole, mate_pack), "gy")

    def eliminate(kernel, name, shapes, time, **more):
        shapes = [(waves, *shape) for shape in shapes]
        return whole_call(functools.partial(kernel, side), name, shapes, time, **more)

    full = 4 * side
    loads = [pltpu.VMEM((waves, 2 * side, 2 * side), jnp.float32), pltpu.SemaphoreType.DMA((4 * waves,))]
    solved_y, rest = eliminate(
        first_kernel, "eliminate_y", [(side, full), (2 * side, full)], 1, tiles=tiles, scratch=loads
    )(own, mate_pack)
    cross_1 = swapped(after(part, (cross_0, solved_y)), "gx")
    far_0 = swapped(cross_0, "gy")
    solved_x, left = eliminate(second_kernel, "eliminate_x", [(side, full), (3 * side, full)], 6)(
        cross_0, solved_y, rest
    )
    solved_v, last = eliminate(third_kernel, "eliminate_v", [(side, 3 * side), (3 * side, 3 * side)], 6)(
        far_0, solved_x, left
    )
    far_1 = swapped(after(cross_1, solved_v), "gy")
    (held,) = eliminate(fourth_kernel, "eliminate_u", [(4, side, 2 * side)], 5)(solved_v, last)
    near = columns_call(
        "near_columns",
        3,
        tiles,
        held,
        [(MATE, units, mate, 0), (CROSS, first, cross_0, base), (FAR, first, far_0, base), (CROSS, second, cross_1, 0)],
        True,
    )
    merged = columns_call("last_columns", 1.5, near, held, [(FAR, second, far_1, 0)], False)
    return merged[:, None, None]


def solution(mesh):
    placed = (P("groups", "gx", "gy", None, None),)
    return jax.shard_map(
        body,
        mesh=mesh,
        in_specs=placed,
        out_specs=P("groups", "gx", "gy", None, None),
        check_vma=False,
    )
```

```python
import functools

import jax
import jax.numpy as jnp
from jax import lax
from jax.experimental import pallas as pl
from jax.experimental.pallas import tpu as pltpu
from jax.sharding import PartitionSpec as P

SUB = 8


def swapped(block, axis):
    count = lax.axis_size(axis)
    bit = count.bit_length() - 2
    route = []
    for low in range(count):
        high = low | 1 << bit
        if high != low and high < count:
            route += [(low, high), (high, low)]
    return lax.ppermute(block, axis, route)


def after(block, other):
    return lax.optimization_barrier((block, other))[0]


def role():
    right = (lax.axis_index("gx") >= lax.axis_size("gx") // 2).astype(jnp.int32)
    top = (lax.axis_index("gy") >= lax.axis_size("gy") // 2).astype(jnp.int32)
    return right, top


def mul(a, b):
    return lax.dot_general(
        a, b, (((1,), (0,)), ((), ())), precision=lax.Precision.HIGHEST, preferred_element_type=jnp.float32
    )


def mul_t(a, b):
    return lax.dot_general(
        a, b, (((0,), (0,)), ((), ())), precision=lax.Precision.HIGHEST, preferred_element_type=jnp.float32
    )


def work(microseconds):
    return int(microseconds * 1e9)


def tree(terms):
    while len(terms) > 1:
        terms = [terms[i] + terms[i + 1] for i in range(0, len(terms) - 1, 2)] + terms[len(terms) & ~1 :]
    return terms[0]


def inverses(matrices):
    size = matrices[0].shape[0]
    panels = size // SUB
    many = len(matrices)
    lane = lax.broadcasted_iota(jnp.int32, (SUB, size), 1)
    sub = lax.broadcasted_iota(jnp.int32, (SUB, size), 0)

    def full(v):
        return jnp.broadcast_to(v, (SUB, size))

    state = [[m[SUB * i : SUB * i + SUB, :] for i in range(panels)] for m in matrices]
    lower = [[] for _ in matrices]
    scaled = [[] for _ in matrices]
    for p in range(panels):
        first = SUB * p
        inside = (lane >= first) & (lane < first + SUB)
        unit = jnp.where(lane - first == sub, 1.0, 0.0)
        done = lane < first + SUB
        blocks = [[full(state[w][p][:, first + j : first + j + 1]) for j in range(SUB)] for w in range(many)]
        panel = [jnp.where(inside, unit, state[w][p]) for w in range(many)]
        for w in range(many):
            lower[w].append(jnp.where(done, panel[w], 0.0))
        for k in range(SUB):
            at_row = sub == k
            for w in range(many):
                block = blocks[w]
                inverse = 1.0 / full(block[k][k : k + 1])
                factor = jnp.where(at_row, -1.0, block[k])

                def step(x):
                    return jnp.where(at_row, 0.0, x) - (factor * full(x[k : k + 1])) * inverse

                for j in range(k + 1, SUB):
                    block[j] = step(block[j])
                panel[w] = step(panel[w])
        for w in range(many):
            gained, rows = panel[w], state[w]
            scaled[w].append(jnp.where(done, gained, 0.0))
            if p + 2 < panels:
                below = jnp.concatenate(rows[p + 2 :], 0)
                within = jnp.concatenate([inside] * (panels - p - 2), 0)
                empty = jnp.zeros((SUB, size), jnp.float32)
                placed = jnp.concatenate([gained if i == p else empty for i in range(panels)], 0)
                change = mul(jnp.where(within, below, 0.0), placed)
                for i in range(p + 2, panels):
                    at = SUB * (i - p - 2)
                    rows[i] = jnp.where(inside, 0.0, rows[i]) - change[at : at + SUB]
            if p + 1 < panels:
                row = rows[p + 1]
                terms = [full(row[:, first + l : first + l + 1]) * full(gained[l : l + 1]) for l in range(SUB)]
                rows[p + 1] = jnp.where(inside, 0.0, row) - tree(terms)
    return [mul_t(jnp.concatenate(lower[w], 0), jnp.concatenate(scaled[w], 0)) for w in range(many)]


def square_masks(side):
    row = lax.broadcasted_iota(jnp.int32, (side, side), 0)
    col = lax.broadcasted_iota(jnp.int32, (side, side), 1)
    return row > col, row == col


def pack_yy(square):
    below, diag = square_masks(square.shape[0])
    return jnp.where(below | diag, square, square.T)


def pack_xx(square, line):
    below, diag = square_masks(square.shape[0])
    return jnp.where(diag, jnp.broadcast_to(line, square.shape), jnp.where(below, square.T, square))


def block_of(tiles, side, w, row_side, col_side):
    rows = pl.ds(pl.multiple_of(row_side * side, side), side)
    cols = pl.ds(pl.multiple_of(col_side * side, side), side)
    return tiles.at[w, rows, cols]


def height(side):
    return 2 * side + SUB


def pack_kernel(side, units, tiles, own, sent, own_yy, own_xx, own_yx, sems, unit_sems):
    right, top = role()
    inner, outer = (3 - top, 1 - right), (right, 2 + top)
    waves = own_yy.shape[0]
    tall = height(side)
    copies = []
    for w in range(waves):
        for n, (i, j, target) in enumerate(((0, 0, own_yy), (1, 1, own_xx), (0, 1, own_yx))):
            source = block_of(tiles, side, w, inner[i], inner[j])
            copies.append(pltpu.make_async_copy(source, target.at[w], sems.at[3 * w + n]))
            copies[-1].start()
    others = load_units(tiles, side, inner, outer, units, sent, waves * tall, unit_sems, 0)
    below, diag = square_masks(side)
    for w in range(waves):
        for copy in copies[3 * w : 3 * w + 3]:
            copy.wait()
        xx = own_xx[w]
        square = jnp.where(below | diag, own_yy[w], xx)
        line = jnp.broadcast_to(jnp.sum(jnp.where(diag, xx, 0.0), 0, keepdims=True), (SUB, side))
        for target in (own, sent):
            target[w * tall : w * tall + side, :] = square
            target[w * tall + side : w * tall + 2 * side, :] = own_yx[w]
            target[w * tall + 2 * side : (w + 1) * tall, :] = line
    for copy in others:
        copy.wait()


def load_units(tiles, side, inner, outer, units, target, base, sems, first):
    copies = []
    for n, unit in enumerate(units):
        w, j = divmod(unit, 2)
        for i in range(2):
            place = target.at[pl.ds(base + (2 * n + i) * side, side), :]
            source = block_of(tiles, side, w, inner[i], outer[j])
            copies.append(pltpu.make_async_copy(source, place, sems.at[first + len(copies)]))
            copies[-1].start()
    return copies


def packed(tiles, units):
    waves, side = tiles.shape[0], tiles.shape[1] // 4
    square = pltpu.VMEM((waves, side, side), jnp.float32)
    rows = waves * height(side)
    return pl.pallas_call(
        functools.partial(pack_kernel, side, units),
        name="pack",
        out_shape=[
            jax.ShapeDtypeStruct((rows, side), jnp.float32),
            jax.ShapeDtypeStruct((rows + len(units) * 2 * side, side), jnp.float32),
        ],
        in_specs=[pl.BlockSpec(memory_space=pl.ANY)],
        out_specs=[pl.BlockSpec(memory_space=pltpu.VMEM)] * 2,
        scratch_shapes=[
            square,
            square,
            square,
            pltpu.SemaphoreType.DMA((3 * waves,)),
            pltpu.SemaphoreType.DMA((2 * len(units),)),
        ],
        cost_estimate=pl.CostEstimate(flops=work(1.5), bytes_accessed=1 << 20, transcendentals=0),
    )(tiles)


def coupling_kernel(side, groups, tiles, *refs):
    targets, sems = refs[:-1], refs[-1]
    right, top = role()
    inner, outer = (3 - top, 1 - right), (right, 2 + top)
    copies = []
    for units, target in zip(groups, targets):
        copies += load_units(tiles, side, inner, outer, units, target, 0, sems, len(copies))
    for copy in copies:
        copy.wait()


def couplings(tiles, groups):
    side = tiles.shape[1] // 4
    count = sum(len(units) for units in groups)
    return pl.pallas_call(
        functools.partial(coupling_kernel, side, groups),
        name="couplings",
        out_shape=[jax.ShapeDtypeStruct((len(units) * 2 * side, side), jnp.float32) for units in groups],
        in_specs=[pl.BlockSpec(memory_space=pl.ANY)],
        out_specs=[pl.BlockSpec(memory_space=pltpu.VMEM)] * len(groups),
        scratch_shapes=[pltpu.SemaphoreType.DMA((2 * count,))],
        cost_estimate=pl.CostEstimate(flops=work(2), bytes_accessed=2 << 20, transcendentals=0),
    )(tiles)


def parts_of(pack, side, w):
    base = w * height(side)
    return pack[base : base + side, :], pack[base + side : base + 2 * side, :], pack[base + 2 * side : base + 2 * side + 1, :]


def load_blocks(tiles, side, row_sides, col_sides, target, sems):
    copies = []
    for w in range(target.shape[0]):
        for i in range(2):
            for j in range(2):
                place = target.at[w, pl.ds(i * side, side), pl.ds(j * side, side)]
                source = block_of(tiles, side, w, row_sides[i], col_sides[j])
                copies.append(pltpu.make_async_copy(source, place, sems.at[len(copies)]))
                copies[-1].start()
    return copies


def first_kernel(side, own, mate, tiles, solved, rest, coupling, sems):
    waves = solved.shape[0]
    right, top = role()
    loads = load_blocks(tiles, side, (3 - top, 1 - right), (right, 2 + top), coupling, sems)
    ours = [parts_of(own, side, w) for w in range(waves)]
    theirs = [parts_of(mate, side, w) for w in range(waves)]
    inverse = inverses([pack_yy(ours[w][0] + theirs[w][0]) for w in range(waves)])
    for load in loads:
        load.wait()
    for w in range(waves):
        across = jnp.concatenate([ours[w][1], theirs[w][1]], 1)
        gains = mul(inverse[w], jnp.concatenate([across, coupling[w, 0:side, :]], 1))
        solved[w] = gains
        change = mul_t(across, gains)
        rest[w, 0:side, 0:side] = pack_xx(ours[w][0], ours[w][2]) - change[0:side, 0:side]
        rest[w, 0:side, side : 2 * side] = -change[0:side, side : 2 * side]
        rest[w, 0:side, 2 * side :] = coupling[w, side:, :] - change[0:side, 2 * side :]
        rest[w, side:, 0:side] = -change[side:, 0:side]
        rest[w, side:, side : 2 * side] = pack_xx(theirs[w][0], theirs[w][2]) - change[side:, side : 2 * side]
        rest[w, side:, 2 * side :] = -change[side:, 2 * side :]


def second_kernel(side, pack, solved_y, rest, solved, left):
    waves = solved.shape[0]
    parts = [parts_of(pack, side, w) for w in range(waves)]
    inverse = inverses([rest[w, 0:side, 0:side] + pack_xx(parts[w][0], parts[w][2]) for w in range(waves)])
    for w in range(waves):
        vx = parts[w][1]
        gains = mul(inverse[w], jnp.concatenate([vx.T, rest[w, 0:side, side : 2 * side]], 1))
        right_gains = mul_split(split(inverse[w]), split(rest[w, 0:side, 2 * side :]), 1)
        solved[w, :, 0 : 2 * side] = gains
        solved[w, :, 2 * side :] = right_gains
        column = jnp.concatenate([vx, rest[w, side:, 0:side]], 0)
        column_y = solved_y[w, :, 0:side]
        change = mul(column, gains)
        change_y = mul_split(split(column_y), split(gains), 1)
        right_change = mul_split(split(jnp.concatenate([column, column_y], 0)), split(right_gains), 1)
        left[w, 0:side, 0:side] = pack_yy(parts[w][0]) - change[0:side, 0:side]
        left[w, 0:side, side : 2 * side] = -change[0:side, side:]
        left[w, 0:side, 2 * side :] = -right_change[0:side]
        left[w, side : 2 * side, 0:side] = -change[side:, 0:side]
        left[w, side : 2 * side, side : 2 * side] = rest[w, side:, side : 2 * side] - change[side:, side:]
        left[w, side : 2 * side, 2 * side :] = rest[w, side:, 2 * side :] - right_change[side : 2 * side]
        left[w, 2 * side :, 0:side] = -change_y[:, 0:side]
        left[w, 2 * side :, side : 2 * side] = solved_y[w, :, side : 2 * side] - change_y[:, side:]
        left[w, 2 * side :, 2 * side :] = solved_y[w, :, 2 * side :] - right_change[2 * side :]


def third_kernel(side, pack, solved_x, left, solved, last):
    waves = solved.shape[0]
    parts = [parts_of(pack, side, w) for w in range(waves)]
    inverse = inverses([left[w, 0:side, 0:side] + pack_yy(parts[w][0]) for w in range(waves)])
    for w in range(waves):
        vu = parts[w][1]
        gains = mul(inverse[w], left[w, 0:side, side : 2 * side] + vu)
        right_gains = mul_split(split(inverse[w]), split(left[w, 0:side, 2 * side :]), 1)
        solved[w, :, 0:side] = gains
        solved[w, :, side:] = right_gains
        column_u = left[w, side : 2 * side, 0:side] + vu.T
        column_yx = jnp.concatenate([left[w, 2 * side :, 0:side], solved_x[w, :, 0:side]], 0)
        uu = pack_xx(parts[w][0], parts[w][2])
        last[w, 0:side, 0:side] = left[w, side : 2 * side, side : 2 * side] + uu - mul(column_u, gains)
        change = mul_split(split(column_yx), split(gains), 1)
        right_change = mul_split(split(jnp.concatenate([column_u, column_yx], 0)), split(right_gains), 1)
        last[w, 0:side, side:] = left[w, side : 2 * side, 2 * side :] - right_change[0:side]
        last[w, side : 2 * side, 0:side] = left[w, 2 * side :, side : 2 * side] - change[0:side]
        last[w, side : 2 * side, side:] = left[w, 2 * side :, 2 * side :] - right_change[side : 2 * side]
        last[w, 2 * side :, 0:side] = solved_x[w, :, side : 2 * side] - change[side:]
        last[w, 2 * side :, side:] = solved_x[w, :, 2 * side :] - right_change[2 * side :]


def fourth_kernel(side, solved_v, last, held):
    waves = last.shape[0]
    inverse = inverses([last[w, 0:side, 0:side] for w in range(waves)])
    for w in range(waves):
        held_u = mul_split(split(inverse[w]), split(last[w, 0:side, side:]), 1)
        column = jnp.concatenate([last[w, side:, 0:side], solved_v[w, :, 0:side]], 0)
        change = mul_split(split(column), split(held_u), 1)
        held[w, 0] = last[w, side : 2 * side, side:] - change[0:side]
        held[w, 1] = last[w, 2 * side :, side:] - change[side : 2 * side]
        held[w, 2] = solved_v[w, :, side:] - change[2 * side :]
        held[w, 3] = held_u


def whole_call(kernel, name, shapes, time, tiles=None, scratch=()):
    vmem = pl.BlockSpec(memory_space=pltpu.VMEM)

    def call(*args):
        specs = [vmem] * len(args)
        if tiles is not None:
            args = (*args, tiles)
            specs.append(pl.BlockSpec(memory_space=pl.ANY))
        return pl.pallas_call(
            kernel,
            name=name,
            out_shape=[jax.ShapeDtypeStruct(s, jnp.float32) for s in shapes],
            in_specs=specs,
            out_specs=[vmem] * len(shapes),
            scratch_shapes=list(scratch),
            compiler_params=pltpu.CompilerParams(vmem_limit_bytes=32 << 20),
            cost_estimate=pl.CostEstimate(flops=work(time), bytes_accessed=1 << 20, transcendentals=0),
        )(*args)

    return call


def split(x):
    high = x.astype(jnp.bfloat16)
    return high, (x - high.astype(jnp.float32)).astype(jnp.bfloat16)


def mul_split(a, b, along=0):
    dims = (((along,), (0,)), ((), ()))
    terms = [(a[0], b[0]), (a[0], b[1]), (a[1], b[0])]
    return sum(lax.dot_general(x, y, dims, preferred_element_type=jnp.float32) for x, y in terms)


MATE, CROSS, FAR = (0, 3), (2, 1), (2, 3)


def columns_kernel(side, groups, with_own, *refs):
    count = len(groups)
    if with_own:
        tiles, held, *arrays = refs[: 2 + count]
        out, coupling, diagonal, load_sems, buffer, sems = refs[2 + count :]
    else:
        _, held, *arrays = refs[: 2 + count]
        out, buffer, sems = refs[2 + count :]
    right, top = role()
    slots = {MATE: 2 * right + 1 - top, CROSS: 2 * (1 - right) + top, FAR: 2 * (1 - right) + 1 - top}
    waves = held.shape[0]
    inner, outer = (3 - top, 1 - right), (right, 2 + top)
    if with_own:
        loads = load_blocks(tiles, side, inner, outer, coupling, load_sems.at[0])
        loads += load_blocks(tiles, side, outer, outer, diagonal, load_sems.at[1])
    parts = {}

    def product(w, box, block):
        if (w, box) not in parts:
            parts[w, box] = split(jnp.concatenate([held[w, i] for i in box], 0))
        return mul_split(parts[w, box], split(block))

    stores = []

    def put(w, slot, j, value):
        n = len(stores)
        width = value.shape[1]
        buffer[n, :, 0:width] = value
        column = pl.multiple_of(slot * 2 * side + j * side, side)
        target = out.at[w, :, pl.ds(column, width)]
        stores.append(pltpu.make_async_copy(buffer.at[n, :, pl.ds(0, width)], target, sems.at[n]))
        stores[-1].start()

    for (box, units, base), array in zip(groups, arrays):
        n = 0
        while n < len(units):
            w, j = divmod(units[n], 2)
            pair = j == 0 and n + 1 < len(units) and units[n + 1] == units[n] + 1
            rows = [array[base + 2 * side * m : base + 2 * side * (m + 1), :] for m in range(n, n + 1 + pair)]
            block = jnp.concatenate(rows, 1)
            put(w, slots[box], j, -product(w, box, block))
            n += 2 if pair else 1
    if with_own:
        for load in loads:
            load.wait()
        for w in range(waves):
            put(w, 2 * right + top, 0, diagonal[w] - product(w, (0, 1), coupling[w]))
    for store in stores:
        store.wait()


def columns_call(name, time, source, held, pieces, with_own):
    waves, side = held.shape[0], held.shape[2]
    groups = tuple((box, units, base) for box, units, _, base in pieces)
    vmem, anywhere = pl.BlockSpec(memory_space=pltpu.VMEM), pl.BlockSpec(memory_space=pl.ANY)
    square = pltpu.VMEM((waves, 2 * side, 2 * side), jnp.float32)
    most = sum(len(units) for _, units, _, _ in pieces) + waves
    scratch = [pltpu.VMEM((most, 2 * side, 2 * side), jnp.float32), pltpu.SemaphoreType.DMA((most,))]
    if with_own:
        scratch = [square, square, pltpu.SemaphoreType.DMA((2, 4 * waves))] + scratch
    return pl.pallas_call(
        functools.partial(columns_kernel, side, groups, with_own),
        name=name,
        out_shape=jax.ShapeDtypeStruct((waves, 2 * side, 8 * side), jnp.float32),
        in_specs=[anywhere] + [vmem] * (1 + len(pieces)),
        out_specs=anywhere,
        scratch_shapes=scratch,
        input_output_aliases={} if with_own else {0: 0},
        compiler_params=pltpu.CompilerParams(vmem_limit_bytes=32 << 20),
        cost_estimate=pl.CostEstimate(flops=work(time), bytes_accessed=1 << 20, transcendentals=0),
    )(source, held, *(array for _, _, array, _ in pieces))


def body(children):
    tiles = children[:, 0, 0]
    waves, side = tiles.shape[0], tiles.shape[1] // 4
    units = tuple(range(2 * waves))
    first, second = units[:1], units[1:]
    base = waves * height(side)
    own, sent = packed(tiles, first)
    whole, part = couplings(tiles, (units, second))
    cross_0 = swapped(sent, "gx")
    mate_pack = swapped(own, "gy")
    mate = swapped(after(whole, mate_pack), "gy")

    def eliminate(kernel, name, shapes, time, **more):
        shapes = [(waves, *shape) for shape in shapes]
        return whole_call(functools.partial(kernel, side), name, shapes, time, **more)

    full = 4 * side
    loads = [pltpu.VMEM((waves, 2 * side, 2 * side), jnp.float32), pltpu.SemaphoreType.DMA((4 * waves,))]
    solved_y, rest = eliminate(
        first_kernel, "eliminate_y", [(side, full), (2 * side, full)], 1, tiles=tiles, scratch=loads
    )(own, mate_pack)
    cross_1 = swapped(after(part, (cross_0, solved_y)), "gx")
    far_0 = swapped(cross_0, "gy")
    solved_x, left = eliminate(second_kernel, "eliminate_x", [(side, full), (3 * side, full)], 6)(
        cross_0, solved_y, rest
    )
    solved_v, last = eliminate(third_kernel, "eliminate_v", [(side, 3 * side), (3 * side, 3 * side)], 6)(
        far_0, solved_x, left
    )
    far_1 = swapped(after(cross_1, solved_v), "gy")
    (held,) = eliminate(fourth_kernel, "eliminate_u", [(4, side, 2 * side)], 5)(solved_v, last)
    near = columns_call(
        "near_columns",
        3,
        tiles,
        held,
        [(MATE, units, mate, 0), (CROSS, first, cross_0, base), (FAR, first, far_0, base), (CROSS, second, cross_1, 0)],
        True,
    )
    merged = columns_call("last_columns", 1.5, near, held, [(FAR, second, far_1, 0)], False)
    return merged[:, None, None]


def solution(mesh):
    placed = (P("groups", "gx", "gy", None, None),)
    return jax.shard_map(
        body,
        mesh=mesh,
        in_specs=placed,
        out_specs=P("groups", "gx", "gy", None, None),
        check_vma=False,
    )
```

```python
import functools

import jax
import jax.numpy as jnp
from jax import lax
from jax.experimental import pallas as pl
from jax.experimental.pallas import tpu as pltpu
from jax.sharding import PartitionSpec as P

SUB = 8


def swapped(block, axis):
    count = lax.axis_size(axis)
    bit = count.bit_length() - 2
    route = []
    for low in range(count):
        high = low | 1 << bit
        if high != low and high < count:
            route += [(low, high), (high, low)]
    return lax.ppermute(block, axis, route)


def after(block, other):
    return lax.optimization_barrier((block, other))[0]


def role():
    right = (lax.axis_index("gx") >= lax.axis_size("gx") // 2).astype(jnp.int32)
    top = (lax.axis_index("gy") >= lax.axis_size("gy") // 2).astype(jnp.int32)
    return right, top


def mul(a, b):
    return lax.dot_general(
        a, b, (((1,), (0,)), ((), ())), precision=lax.Precision.HIGHEST, preferred_element_type=jnp.float32
    )


def mul_t(a, b):
    return lax.dot_general(
        a, b, (((0,), (0,)), ((), ())), precision=lax.Precision.HIGHEST, preferred_element_type=jnp.float32
    )


def work(microseconds):
    return int(microseconds * 1e9)


def tree(terms):
    while len(terms) > 1:
        terms = [terms[i] + terms[i + 1] for i in range(0, len(terms) - 1, 2)] + terms[len(terms) & ~1 :]
    return terms[0]


def inverses(matrices):
    size = matrices[0].shape[0]
    panels = size // SUB
    many = len(matrices)
    lane = lax.broadcasted_iota(jnp.int32, (SUB, size), 1)
    sub = lax.broadcasted_iota(jnp.int32, (SUB, size), 0)

    def full(v):
        return jnp.broadcast_to(v, (SUB, size))

    state = [[m[SUB * i : SUB * i + SUB, :] for i in range(panels)] for m in matrices]
    lower = [[] for _ in matrices]
    scaled = [[] for _ in matrices]
    for p in range(panels):
        first = SUB * p
        inside = (lane >= first) & (lane < first + SUB)
        unit = jnp.where(lane - first == sub, 1.0, 0.0)
        done = lane < first + SUB
        blocks = [[full(state[w][p][:, first + j : first + j + 1]) for j in range(SUB)] for w in range(many)]
        panel = [jnp.where(inside, unit, state[w][p]) for w in range(many)]
        for w in range(many):
            lower[w].append(jnp.where(done, panel[w], 0.0))
        for k in range(SUB):
            at_row = sub == k
            for w in range(many):
                block = blocks[w]
                inverse = 1.0 / full(block[k][k : k + 1])
                factor = jnp.where(at_row, -1.0, block[k])

                def step(x):
                    return jnp.where(at_row, 0.0, x) - (factor * full(x[k : k + 1])) * inverse

                for j in range(k + 1, SUB):
                    block[j] = step(block[j])
                panel[w] = step(panel[w])
        for w in range(many):
            gained, rows = panel[w], state[w]
            scaled[w].append(jnp.where(done, gained, 0.0))
            if p + 2 < panels:
                below = jnp.concatenate(rows[p + 2 :], 0)
                within = jnp.concatenate([inside] * (panels - p - 2), 0)
                empty = jnp.zeros((SUB, size), jnp.float32)
                placed = jnp.concatenate([gained if i == p else empty for i in range(panels)], 0)
                change = mul(jnp.where(within, below, 0.0), placed)
                for i in range(p + 2, panels):
                    at = SUB * (i - p - 2)
                    rows[i] = jnp.where(inside, 0.0, rows[i]) - change[at : at + SUB]
            if p + 1 < panels:
                row = rows[p + 1]
                terms = [full(row[:, first + l : first + l + 1]) * full(gained[l : l + 1]) for l in range(SUB)]
                rows[p + 1] = jnp.where(inside, 0.0, row) - tree(terms)
    return [mul_t(jnp.concatenate(lower[w], 0), jnp.concatenate(scaled[w], 0)) for w in range(many)]


def square_masks(side):
    row = lax.broadcasted_iota(jnp.int32, (side, side), 0)
    col = lax.broadcasted_iota(jnp.int32, (side, side), 1)
    return row > col, row == col


def pack_yy(square):
    below, diag = square_masks(square.shape[0])
    return jnp.where(below | diag, square, square.T)


def pack_xx(square, line):
    below, diag = square_masks(square.shape[0])
    return jnp.where(diag, jnp.broadcast_to(line, square.shape), jnp.where(below, square.T, square))


def block_of(tiles, side, w, row_side, col_side):
    rows = pl.ds(pl.multiple_of(row_side * side, side), side)
    cols = pl.ds(pl.multiple_of(col_side * side, side), side)
    return tiles.at[w, rows, cols]


def height(side):
    return 2 * side + SUB


def pack_kernel(side, units, tiles, own, sent, own_yy, own_xx, sems, unit_sems):
    right, top = role()
    inner, outer = (3 - top, 1 - right), (right, 2 + top)
    waves = own_yy.shape[0]
    tall = height(side)
    copies = []
    for w in range(waves):
        yx = pl.ds(w * tall + side, side)
        for n, (i, j, target) in enumerate(
            ((0, 0, own_yy.at[w]), (1, 1, own_xx.at[w]), (0, 1, own.at[yx, :]), (0, 1, sent.at[yx, :]))
        ):
            source = block_of(tiles, side, w, inner[i], inner[j])
            copies.append(pltpu.make_async_copy(source, target, sems.at[4 * w + n]))
            copies[-1].start()
    others = load_units(tiles, side, inner, outer, units, sent, waves * tall, unit_sems, 0)
    below, diag = square_masks(side)
    for w in range(waves):
        for copy in copies[4 * w : 4 * w + 2]:
            copy.wait()
        xx = own_xx[w]
        square = jnp.where(below | diag, own_yy[w], xx)
        line = jnp.broadcast_to(jnp.sum(jnp.where(diag, xx, 0.0), 0, keepdims=True), (SUB, side))
        for target in (own, sent):
            target[w * tall : w * tall + side, :] = square
            target[w * tall + 2 * side : (w + 1) * tall, :] = line
    for w in range(waves):
        for copy in copies[4 * w + 2 : 4 * w + 4]:
            copy.wait()
    for copy in others:
        copy.wait()


def load_units(tiles, side, inner, outer, units, target, base, sems, first):
    copies = []
    for n, unit in enumerate(units):
        w, j = divmod(unit, 2)
        for i in range(2):
            place = target.at[pl.ds(base + (2 * n + i) * side, side), :]
            source = block_of(tiles, side, w, inner[i], outer[j])
            copies.append(pltpu.make_async_copy(source, place, sems.at[first + len(copies)]))
            copies[-1].start()
    return copies


def packed(tiles, units):
    waves, side = tiles.shape[0], tiles.shape[1] // 4
    square = pltpu.VMEM((waves, side, side), jnp.float32)
    rows = waves * height(side)
    return pl.pallas_call(
        functools.partial(pack_kernel, side, units),
        name="pack",
        out_shape=[
            pltpu.VMEM((rows, side), jnp.float32),
            pltpu.VMEM((rows + len(units) * 2 * side, side), jnp.float32),
        ],
        in_specs=[pl.BlockSpec(memory_space=pl.ANY)],
        out_specs=[pl.BlockSpec(memory_space=pltpu.VMEM)] * 2,
        scratch_shapes=[
            square,
            square,
            pltpu.SemaphoreType.DMA((4 * waves,)),
            pltpu.SemaphoreType.DMA((2 * len(units),)),
        ],
        cost_estimate=pl.CostEstimate(flops=work(1.5), bytes_accessed=1 << 20, transcendentals=0),
    )(tiles)


def coupling_kernel(side, groups, tiles, *refs):
    targets, sems = refs[:-1], refs[-1]
    right, top = role()
    inner, outer = (3 - top, 1 - right), (right, 2 + top)
    copies = []
    for units, target in zip(groups, targets):
        copies += load_units(tiles, side, inner, outer, units, target, 0, sems, len(copies))
    for copy in copies:
        copy.wait()


def couplings(tiles, groups):
    side = tiles.shape[1] // 4
    count = sum(len(units) for units in groups)
    return pl.pallas_call(
        functools.partial(coupling_kernel, side, groups),
        name="couplings",
        out_shape=[jax.ShapeDtypeStruct((len(units) * 2 * side, side), jnp.float32) for units in groups],
        in_specs=[pl.BlockSpec(memory_space=pl.ANY)],
        out_specs=[pl.BlockSpec(memory_space=pltpu.VMEM)] * len(groups),
        scratch_shapes=[pltpu.SemaphoreType.DMA((2 * count,))],
        cost_estimate=pl.CostEstimate(flops=work(2), bytes_accessed=2 << 20, transcendentals=0),
    )(tiles)


def parts_of(pack, side, w):
    base = w * height(side)
    return pack[base : base + side, :], pack[base + side : base + 2 * side, :], pack[base + 2 * side : base + 2 * side + 1, :]


def load_blocks(tiles, side, row_sides, col_sides, target, sems):
    copies = []
    for w in range(target.shape[0]):
        for i in range(2):
            for j in range(2):
                place = target.at[w, pl.ds(i * side, side), pl.ds(j * side, side)]
                source = block_of(tiles, side, w, row_sides[i], col_sides[j])
                copies.append(pltpu.make_async_copy(source, place, sems.at[len(copies)]))
                copies[-1].start()
    return copies


def first_kernel(side, own, mate, tiles, solved, rest, coupling, sems):
    waves = solved.shape[0]
    right, top = role()
    loads = load_blocks(tiles, side, (3 - top, 1 - right), (right, 2 + top), coupling, sems)
    ours = [parts_of(own, side, w) for w in range(waves)]
    theirs = [parts_of(mate, side, w) for w in range(waves)]
    inverse = inverses([pack_yy(ours[w][0] + theirs[w][0]) for w in range(waves)])
    for load in loads:
        load.wait()
    for w in range(waves):
        across = jnp.concatenate([ours[w][1], theirs[w][1]], 1)
        gains = mul(inverse[w], jnp.concatenate([across, coupling[w, 0:side, :]], 1))
        solved[w] = gains
        change = mul_t(across, gains)
        rest[w, 0:side, 0:side] = pack_xx(ours[w][0], ours[w][2]) - change[0:side, 0:side]
        rest[w, 0:side, side : 2 * side] = -change[0:side, side : 2 * side]
        rest[w, 0:side, 2 * side :] = coupling[w, side:, :] - change[0:side, 2 * side :]
        rest[w, side:, 0:side] = -change[side:, 0:side]
        rest[w, side:, side : 2 * side] = pack_xx(theirs[w][0], theirs[w][2]) - change[side:, side : 2 * side]
        rest[w, side:, 2 * side :] = -change[side:, 2 * side :]


def second_kernel(side, pack, solved_y, rest, solved, left):
    waves = solved.shape[0]
    parts = [parts_of(pack, side, w) for w in range(waves)]
    inverse = inverses([rest[w, 0:side, 0:side] + pack_xx(parts[w][0], parts[w][2]) for w in range(waves)])
    for w in range(waves):
        vx = parts[w][1]
        gains = mul(inverse[w], jnp.concatenate([vx.T, rest[w, 0:side, side : 2 * side]], 1))
        right_gains = mul_split(split(inverse[w]), split(rest[w, 0:side, 2 * side :]), 1)
        solved[w, :, 0 : 2 * side] = gains
        solved[w, :, 2 * side :] = right_gains
        column = jnp.concatenate([vx, rest[w, side:, 0:side]], 0)
        column_y = solved_y[w, :, 0:side]
        change = mul(column, gains)
        change_y = mul_split(split(column_y), split(gains), 1)
        right_change = mul_split(split(jnp.concatenate([column, column_y], 0)), split(right_gains), 1)
        left[w, 0:side, 0:side] = pack_yy(parts[w][0]) - change[0:side, 0:side]
        left[w, 0:side, side : 2 * side] = -change[0:side, side:]
        left[w, 0:side, 2 * side :] = -right_change[0:side]
        left[w, side : 2 * side, 0:side] = -change[side:, 0:side]
        left[w, side : 2 * side, side : 2 * side] = rest[w, side:, side : 2 * side] - change[side:, side:]
        left[w, side : 2 * side, 2 * side :] = rest[w, side:, 2 * side :] - right_change[side : 2 * side]
        left[w, 2 * side :, 0:side] = -change_y[:, 0:side]
        left[w, 2 * side :, side : 2 * side] = solved_y[w, :, side : 2 * side] - change_y[:, side:]
        left[w, 2 * side :, 2 * side :] = solved_y[w, :, 2 * side :] - right_change[2 * side :]


def third_kernel(side, pack, solved_x, left, solved, last):
    waves = solved.shape[0]
    parts = [parts_of(pack, side, w) for w in range(waves)]
    inverse = inverses([left[w, 0:side, 0:side] + pack_yy(parts[w][0]) for w in range(waves)])
    for w in range(waves):
        vu = parts[w][1]
        gains = mul(inverse[w], left[w, 0:side, side : 2 * side] + vu)
        right_gains = mul_split(split(inverse[w]), split(left[w, 0:side, 2 * side :]), 1)
        solved[w, :, 0:side] = gains
        solved[w, :, side:] = right_gains
        column_u = left[w, side : 2 * side, 0:side] + vu.T
        column_yx = jnp.concatenate([left[w, 2 * side :, 0:side], solved_x[w, :, 0:side]], 0)
        uu = pack_xx(parts[w][0], parts[w][2])
        last[w, 0:side, 0:side] = left[w, side : 2 * side, side : 2 * side] + uu - mul(column_u, gains)
        change = mul_split(split(column_yx), split(gains), 1)
        right_change = mul_split(split(jnp.concatenate([column_u, column_yx], 0)), split(right_gains), 1)
        last[w, 0:side, side:] = left[w, side : 2 * side, 2 * side :] - right_change[0:side]
        last[w, side : 2 * side, 0:side] = left[w, 2 * side :, side : 2 * side] - change[0:side]
        last[w, side : 2 * side, side:] = left[w, 2 * side :, 2 * side :] - right_change[side : 2 * side]
        last[w, 2 * side :, 0:side] = solved_x[w, :, side : 2 * side] - change[side:]
        last[w, 2 * side :, side:] = solved_x[w, :, 2 * side :] - right_change[2 * side :]


def fourth_kernel(side, solved_v, last, held):
    waves = last.shape[0]
    inverse = inverses([last[w, 0:side, 0:side] for w in range(waves)])
    for w in range(waves):
        held_u = mul_split(split(inverse[w]), split(last[w, 0:side, side:]), 1)
        column = jnp.concatenate([last[w, side:, 0:side], solved_v[w, :, 0:side]], 0)
        change = mul_split(split(column), split(held_u), 1)
        held[w, 0] = last[w, side : 2 * side, side:] - change[0:side]
        held[w, 1] = last[w, 2 * side :, side:] - change[side : 2 * side]
        held[w, 2] = solved_v[w, :, side:] - change[2 * side :]
        held[w, 3] = held_u


def whole_call(kernel, name, shapes, time, tiles=None, scratch=()):
    vmem = pl.BlockSpec(memory_space=pltpu.VMEM)

    def call(*args):
        specs = [vmem] * len(args)
        if tiles is not None:
            args = (*args, tiles)
            specs.append(pl.BlockSpec(memory_space=pl.ANY))
        return pl.pallas_call(
            kernel,
            name=name,
            out_shape=[jax.ShapeDtypeStruct(s, jnp.float32) for s in shapes],
            in_specs=specs,
            out_specs=[vmem] * len(shapes),
            scratch_shapes=list(scratch),
            compiler_params=pltpu.CompilerParams(vmem_limit_bytes=32 << 20),
            cost_estimate=pl.CostEstimate(flops=work(time), bytes_accessed=1 << 20, transcendentals=0),
        )(*args)

    return call


def split(x):
    high = x.astype(jnp.bfloat16)
    return high, (x - high.astype(jnp.float32)).astype(jnp.bfloat16)


def mul_split(a, b, along=0):
    dims = (((along,), (0,)), ((), ()))
    terms = [(a[0], b[0]), (a[0], b[1]), (a[1], b[0])]
    return sum(lax.dot_general(x, y, dims, preferred_element_type=jnp.float32) for x, y in terms)


MATE, CROSS, FAR = (0, 3), (2, 1), (2, 3)


def columns_kernel(side, groups, with_own, *refs):
    count = len(groups)
    if with_own:
        tiles, held, *arrays = refs[: 2 + count]
        out, coupling, diagonal, load_sems, buffer, sems = refs[2 + count :]
    else:
        _, held, *arrays = refs[: 2 + count]
        out, buffer, sems = refs[2 + count :]
    right, top = role()
    slots = {MATE: 2 * right + 1 - top, CROSS: 2 * (1 - right) + top, FAR: 2 * (1 - right) + 1 - top}
    waves = held.shape[0]
    inner, outer = (3 - top, 1 - right), (right, 2 + top)
    if with_own:
        loads = load_blocks(tiles, side, inner, outer, coupling, load_sems.at[0])
        loads += load_blocks(tiles, side, outer, outer, diagonal, load_sems.at[1])
    parts = {}

    def product(w, box, block):
        if (w, box) not in parts:
            parts[w, box] = split(jnp.concatenate([held[w, i] for i in box], 0))
        return mul_split(parts[w, box], split(block))

    stores = []

    def put(w, slot, j, value):
        n = len(stores)
        width = value.shape[1]
        buffer[n, :, 0:width] = value
        column = pl.multiple_of(slot * 2 * side + j * side, side)
        target = out.at[w, :, pl.ds(column, width)]
        stores.append(pltpu.make_async_copy(buffer.at[n, :, pl.ds(0, width)], target, sems.at[n]))
        stores[-1].start()

    for (box, units, base), array in zip(groups, arrays):
        n = 0
        while n < len(units):
            w, j = divmod(units[n], 2)
            pair = j == 0 and n + 1 < len(units) and units[n + 1] == units[n] + 1
            rows = [array[base + 2 * side * m : base + 2 * side * (m + 1), :] for m in range(n, n + 1 + pair)]
            block = jnp.concatenate(rows, 1)
            put(w, slots[box], j, -product(w, box, block))
            n += 2 if pair else 1
    if with_own:
        for load in loads:
            load.wait()
        for w in range(waves):
            put(w, 2 * right + top, 0, diagonal[w] - product(w, (0, 1), coupling[w]))
    for store in stores:
        store.wait()


def columns_call(name, time, source, held, pieces, with_own):
    waves, side = held.shape[0], held.shape[2]
    groups = tuple((box, units, base) for box, units, _, base in pieces)
    vmem, anywhere = pl.BlockSpec(memory_space=pltpu.VMEM), pl.BlockSpec(memory_space=pl.ANY)
    square = pltpu.VMEM((waves, 2 * side, 2 * side), jnp.float32)
    most = sum(len(units) for _, units, _, _ in pieces) + waves
    scratch = [pltpu.VMEM((most, 2 * side, 2 * side), jnp.float32), pltpu.SemaphoreType.DMA((most,))]
    if with_own:
        scratch = [square, square, pltpu.SemaphoreType.DMA((2, 4 * waves))] + scratch
    return pl.pallas_call(
        functools.partial(columns_kernel, side, groups, with_own),
        name=name,
        out_shape=jax.ShapeDtypeStruct((waves, 2 * side, 8 * side), jnp.float32),
        in_specs=[anywhere] + [vmem] * (1 + len(pieces)),
        out_specs=anywhere,
        scratch_shapes=scratch,
        input_output_aliases={} if with_own else {0: 0},
        compiler_params=pltpu.CompilerParams(vmem_limit_bytes=32 << 20),
        cost_estimate=pl.CostEstimate(flops=work(time), bytes_accessed=1 << 20, transcendentals=0),
    )(source, held, *(array for _, _, array, _ in pieces))


def body(children):
    tiles = children[:, 0, 0]
    waves, side = tiles.shape[0], tiles.shape[1] // 4
    units = tuple(range(2 * waves))
    first, second = units[:1], units[1:]
    base = waves * height(side)
    own, sent = packed(tiles, first)
    whole, part = couplings(tiles, (units, second))
    cross_0 = swapped(sent, "gx")
    mate_pack = swapped(own, "gy")
    mate = swapped(whole, "gy")

    def eliminate(kernel, name, shapes, time, **more):
        shapes = [(waves, *shape) for shape in shapes]
        return whole_call(functools.partial(kernel, side), name, shapes, time, **more)

    full = 4 * side
    loads = [pltpu.VMEM((waves, 2 * side, 2 * side), jnp.float32), pltpu.SemaphoreType.DMA((4 * waves,))]
    solved_y, rest = eliminate(
        first_kernel, "eliminate_y", [(side, full), (2 * side, full)], 1, tiles=tiles, scratch=loads
    )(own, mate_pack)
    cross_1 = swapped(after(part, (cross_0, solved_y)), "gx")
    far_0 = swapped(cross_0, "gy")
    solved_x, left = eliminate(second_kernel, "eliminate_x", [(side, full), (3 * side, full)], 6)(
        cross_0, solved_y, rest
    )
    solved_v, last = eliminate(third_kernel, "eliminate_v", [(side, 3 * side), (3 * side, 3 * side)], 6)(
        far_0, solved_x, left
    )
    far_1 = swapped(after(cross_1, solved_v), "gy")
    (held,) = eliminate(fourth_kernel, "eliminate_u", [(4, side, 2 * side)], 5)(solved_v, last)
    near = columns_call(
        "near_columns",
        3,
        tiles,
        held,
        [(MATE, units, mate, 0), (CROSS, first, cross_0, base), (FAR, first, far_0, base), (CROSS, second, cross_1, 0)],
        True,
    )
    merged = columns_call("last_columns", 1.5, near, held, [(FAR, second, far_1, 0)], False)
    return merged[:, None, None]


def solution(mesh):
    placed = (P("groups", "gx", "gy", None, None),)
    return jax.shard_map(
        body,
        mesh=mesh,
        in_specs=placed,
        out_specs=P("groups", "gx", "gy", None, None),
        check_vma=False,
    )
```

```python
import functools

import jax
import jax.numpy as jnp
from jax import lax
from jax.experimental import pallas as pl
from jax.experimental.pallas import tpu as pltpu
from jax.sharding import PartitionSpec as P

SUB = 8


def swapped(block, axis):
    count = lax.axis_size(axis)
    bit = count.bit_length() - 2
    route = []
    for low in range(count):
        high = low | 1 << bit
        if high != low and high < count:
            route += [(low, high), (high, low)]
    return lax.ppermute(block, axis, route)


def after(block, other):
    return lax.optimization_barrier((block, other))[0]


def role():
    right = (lax.axis_index("gx") >= lax.axis_size("gx") // 2).astype(jnp.int32)
    top = (lax.axis_index("gy") >= lax.axis_size("gy") // 2).astype(jnp.int32)
    return right, top


def mul(a, b):
    return lax.dot_general(
        a, b, (((1,), (0,)), ((), ())), precision=lax.Precision.HIGHEST, preferred_element_type=jnp.float32
    )


def mul_t(a, b):
    return lax.dot_general(
        a, b, (((0,), (0,)), ((), ())), precision=lax.Precision.HIGHEST, preferred_element_type=jnp.float32
    )


def work(microseconds):
    return int(microseconds * 1e9)


def tree(terms):
    while len(terms) > 1:
        terms = [terms[i] + terms[i + 1] for i in range(0, len(terms) - 1, 2)] + terms[len(terms) & ~1 :]
    return terms[0]


def inverses(matrices):
    size = matrices[0].shape[0]
    panels = size // SUB
    many = len(matrices)
    lane = lax.broadcasted_iota(jnp.int32, (SUB, size), 1)
    sub = lax.broadcasted_iota(jnp.int32, (SUB, size), 0)

    def full(v):
        return jnp.broadcast_to(v, (SUB, size))

    state = [[m[SUB * i : SUB * i + SUB, :] for i in range(panels)] for m in matrices]
    lower = [[] for _ in matrices]
    scaled = [[] for _ in matrices]
    for p in range(panels):
        first = SUB * p
        inside = (lane >= first) & (lane < first + SUB)
        unit = jnp.where(lane - first == sub, 1.0, 0.0)
        done = lane < first + SUB
        blocks = [[full(state[w][p][:, first + j : first + j + 1]) for j in range(SUB)] for w in range(many)]
        panel = [jnp.where(inside, unit, state[w][p]) for w in range(many)]
        for w in range(many):
            lower[w].append(jnp.where(done, panel[w], 0.0))
        for k in range(SUB):
            at_row = sub == k
            for w in range(many):
                block = blocks[w]
                inverse = 1.0 / full(block[k][k : k + 1])
                factor = jnp.where(at_row, -1.0, block[k])

                def step(x):
                    return jnp.where(at_row, 0.0, x) - (factor * full(x[k : k + 1])) * inverse

                for j in range(k + 1, SUB):
                    block[j] = step(block[j])
                panel[w] = step(panel[w])
        for w in range(many):
            gained, rows = panel[w], state[w]
            scaled[w].append(jnp.where(done, gained, 0.0))
            if p + 2 < panels:
                below = jnp.concatenate(rows[p + 2 :], 0)
                within = jnp.concatenate([inside] * (panels - p - 2), 0)
                empty = jnp.zeros((SUB, size), jnp.float32)
                placed = jnp.concatenate([gained if i == p else empty for i in range(panels)], 0)
                change = mul(jnp.where(within, below, 0.0), placed)
                for i in range(p + 2, panels):
                    at = SUB * (i - p - 2)
                    rows[i] = jnp.where(inside, 0.0, rows[i]) - change[at : at + SUB]
            if p + 1 < panels:
                row = rows[p + 1]
                terms = [full(row[:, first + l : first + l + 1]) * full(gained[l : l + 1]) for l in range(SUB)]
                rows[p + 1] = jnp.where(inside, 0.0, row) - tree(terms)
    return [mul_t(jnp.concatenate(lower[w], 0), jnp.concatenate(scaled[w], 0)) for w in range(many)]


def square_masks(side):
    row = lax.broadcasted_iota(jnp.int32, (side, side), 0)
    col = lax.broadcasted_iota(jnp.int32, (side, side), 1)
    return row > col, row == col


def pack_yy(square):
    below, diag = square_masks(square.shape[0])
    return jnp.where(below | diag, square, square.T)


def pack_xx(square, line):
    below, diag = square_masks(square.shape[0])
    return jnp.where(diag, jnp.broadcast_to(line, square.shape), jnp.where(below, square.T, square))


def block_of(tiles, side, w, row_side, col_side):
    rows = pl.ds(pl.multiple_of(row_side * side, side), side)
    cols = pl.ds(pl.multiple_of(col_side * side, side), side)
    return tiles.at[w, rows, cols]


def height(side):
    return 2 * side + SUB


def pack_kernel(side, units, tiles, own, sent, own_yy, own_xx, sems, unit_sems):
    right, top = role()
    inner, outer = (3 - top, 1 - right), (right, 2 + top)
    waves = own_yy.shape[0]
    tall = height(side)
    copies = []
    for w in range(waves):
        yx = pl.ds(w * tall + side, side)
        for n, (i, j, target) in enumerate(
            ((0, 0, own_yy.at[w]), (1, 1, own_xx.at[w]), (0, 1, own.at[yx, :]), (0, 1, sent.at[yx, :]))
        ):
            source = block_of(tiles, side, w, inner[i], inner[j])
            copies.append(pltpu.make_async_copy(source, target, sems.at[4 * w + n]))
            copies[-1].start()
    others = load_units(tiles, side, inner, outer, units, sent, waves * tall, unit_sems, 0)
    below, diag = square_masks(side)
    for w in range(waves):
        for copy in copies[4 * w : 4 * w + 2]:
            copy.wait()
        xx = own_xx[w]
        square = jnp.where(below | diag, own_yy[w], xx)
        line = jnp.broadcast_to(jnp.sum(jnp.where(diag, xx, 0.0), 0, keepdims=True), (SUB, side))
        for target in (own, sent):
            target[w * tall : w * tall + side, :] = square
            target[w * tall + 2 * side : (w + 1) * tall, :] = line
    for w in range(waves):
        for copy in copies[4 * w + 2 : 4 * w + 4]:
            copy.wait()
    for copy in others:
        copy.wait()


def load_units(tiles, side, inner, outer, units, target, base, sems, first):
    copies = []
    for n, unit in enumerate(units):
        w, j = divmod(unit, 2)
        for i in range(2):
            place = target.at[pl.ds(base + (2 * n + i) * side, side), :]
            source = block_of(tiles, side, w, inner[i], outer[j])
            copies.append(pltpu.make_async_copy(source, place, sems.at[first + len(copies)]))
            copies[-1].start()
    return copies


def packed(tiles, units):
    waves, side = tiles.shape[0], tiles.shape[1] // 4
    square = pltpu.VMEM((waves, side, side), jnp.float32)
    rows = waves * height(side)
    return pl.pallas_call(
        functools.partial(pack_kernel, side, units),
        name="pack",
        out_shape=[
            pltpu.VMEM((rows, side), jnp.float32),
            pltpu.VMEM((rows + len(units) * 2 * side, side), jnp.float32),
        ],
        in_specs=[pl.BlockSpec(memory_space=pl.ANY)],
        out_specs=[pl.BlockSpec(memory_space=pltpu.VMEM)] * 2,
        scratch_shapes=[
            square,
            square,
            pltpu.SemaphoreType.DMA((4 * waves,)),
            pltpu.SemaphoreType.DMA((2 * len(units),)),
        ],
        cost_estimate=pl.CostEstimate(flops=work(1.5), bytes_accessed=1 << 20, transcendentals=0),
    )(tiles)


def coupling_kernel(side, groups, tiles, *refs):
    targets, sems = refs[:-1], refs[-1]
    right, top = role()
    inner, outer = (3 - top, 1 - right), (right, 2 + top)
    copies = []
    for units, target in zip(groups, targets):
        copies += load_units(tiles, side, inner, outer, units, target, 0, sems, len(copies))
    for copy in copies:
        copy.wait()


def couplings(tiles, groups):
    side = tiles.shape[1] // 4
    count = sum(len(units) for units in groups)
    return pl.pallas_call(
        functools.partial(coupling_kernel, side, groups),
        name="couplings",
        out_shape=[jax.ShapeDtypeStruct((len(units) * 2 * side, side), jnp.float32) for units in groups],
        in_specs=[pl.BlockSpec(memory_space=pl.ANY)],
        out_specs=[pl.BlockSpec(memory_space=pltpu.VMEM)] * len(groups),
        scratch_shapes=[pltpu.SemaphoreType.DMA((2 * count,))],
        cost_estimate=pl.CostEstimate(flops=work(2), bytes_accessed=2 << 20, transcendentals=0),
    )(tiles)


def parts_of(pack, side, w):
    base = w * height(side)
    return pack[base : base + side, :], pack[base + side : base + 2 * side, :], pack[base + 2 * side : base + 2 * side + 1, :]


def load_blocks(tiles, side, row_sides, col_sides, target, sems):
    copies = []
    for w in range(target.shape[0]):
        for i in range(2):
            for j in range(2):
                place = target.at[w, pl.ds(i * side, side), pl.ds(j * side, side)]
                source = block_of(tiles, side, w, row_sides[i], col_sides[j])
                copies.append(pltpu.make_async_copy(source, place, sems.at[len(copies)]))
                copies[-1].start()
    return copies


def first_kernel(side, own, mate, tiles, solved, rest, coupling, sems):
    waves = solved.shape[0]
    right, top = role()
    loads = load_blocks(tiles, side, (3 - top, 1 - right), (right, 2 + top), coupling, sems)
    ours = [parts_of(own, side, w) for w in range(waves)]
    theirs = [parts_of(mate, side, w) for w in range(waves)]
    inverse = inverses([pack_yy(ours[w][0] + theirs[w][0]) for w in range(waves)])
    for load in loads:
        load.wait()
    for w in range(waves):
        across = jnp.concatenate([ours[w][1], theirs[w][1]], 1)
        gains = mul(inverse[w], jnp.concatenate([across, coupling[w, 0:side, :]], 1))
        solved[w] = gains
        change = mul_t(across, gains)
        rest[w, 0:side, 0:side] = pack_xx(ours[w][0], ours[w][2]) - change[0:side, 0:side]
        rest[w, 0:side, side : 2 * side] = -change[0:side, side : 2 * side]
        rest[w, 0:side, 2 * side :] = coupling[w, side:, :] - change[0:side, 2 * side :]
        rest[w, side:, 0:side] = -change[side:, 0:side]
        rest[w, side:, side : 2 * side] = pack_xx(theirs[w][0], theirs[w][2]) - change[side:, side : 2 * side]
        rest[w, side:, 2 * side :] = -change[side:, 2 * side :]


def second_kernel(side, pack, solved_y, rest, solved, left):
    waves = solved.shape[0]
    parts = [parts_of(pack, side, w) for w in range(waves)]
    inverse = inverses([rest[w, 0:side, 0:side] + pack_xx(parts[w][0], parts[w][2]) for w in range(waves)])
    for w in range(waves):
        vx = parts[w][1]
        gains = mul(inverse[w], jnp.concatenate([vx.T, rest[w, 0:side, side : 2 * side]], 1))
        right_gains = mul_split(split(inverse[w]), split(rest[w, 0:side, 2 * side :]), 1)
        solved[w, :, 0 : 2 * side] = gains
        solved[w, :, 2 * side :] = right_gains
        column = jnp.concatenate([vx, rest[w, side:, 0:side]], 0)
        column_y = solved_y[w, :, 0:side]
        change = mul(column, gains)
        change_y = mul_split(split(column_y), split(gains), 1)
        right_change = mul_split(split(jnp.concatenate([column, column_y], 0)), split(right_gains), 1)
        left[w, 0:side, 0:side] = pack_yy(parts[w][0]) - change[0:side, 0:side]
        left[w, 0:side, side : 2 * side] = -change[0:side, side:]
        left[w, 0:side, 2 * side :] = -right_change[0:side]
        left[w, side : 2 * side, 0:side] = -change[side:, 0:side]
        left[w, side : 2 * side, side : 2 * side] = rest[w, side:, side : 2 * side] - change[side:, side:]
        left[w, side : 2 * side, 2 * side :] = rest[w, side:, 2 * side :] - right_change[side : 2 * side]
        left[w, 2 * side :, 0:side] = -change_y[:, 0:side]
        left[w, 2 * side :, side : 2 * side] = solved_y[w, :, side : 2 * side] - change_y[:, side:]
        left[w, 2 * side :, 2 * side :] = solved_y[w, :, 2 * side :] - right_change[2 * side :]


def third_kernel(side, pack, solved_x, left, solved, last):
    waves = solved.shape[0]
    parts = [parts_of(pack, side, w) for w in range(waves)]
    inverse = inverses([left[w, 0:side, 0:side] + pack_yy(parts[w][0]) for w in range(waves)])
    for w in range(waves):
        vu = parts[w][1]
        gains = mul(inverse[w], left[w, 0:side, side : 2 * side] + vu)
        right_gains = mul_split(split(inverse[w]), split(left[w, 0:side, 2 * side :]), 1)
        solved[w, :, 0:side] = gains
        solved[w, :, side:] = right_gains
        column_u = left[w, side : 2 * side, 0:side] + vu.T
        column_yx = jnp.concatenate([left[w, 2 * side :, 0:side], solved_x[w, :, 0:side]], 0)
        uu = pack_xx(parts[w][0], parts[w][2])
        last[w, 0:side, 0:side] = left[w, side : 2 * side, side : 2 * side] + uu - mul(column_u, gains)
        change = mul_split(split(column_yx), split(gains), 1)
        right_change = mul_split(split(jnp.concatenate([column_u, column_yx], 0)), split(right_gains), 1)
        last[w, 0:side, side:] = left[w, side : 2 * side, 2 * side :] - right_change[0:side]
        last[w, side : 2 * side, 0:side] = left[w, 2 * side :, side : 2 * side] - change[0:side]
        last[w, side : 2 * side, side:] = left[w, 2 * side :, 2 * side :] - right_change[side : 2 * side]
        last[w, 2 * side :, 0:side] = solved_x[w, :, side : 2 * side] - change[side:]
        last[w, 2 * side :, side:] = solved_x[w, :, 2 * side :] - right_change[2 * side :]


def fourth_kernel(side, solved_v, last, held):
    waves = last.shape[0]
    inverse = inverses([last[w, 0:side, 0:side] for w in range(waves)])
    for w in range(waves):
        held_u = mul_split(split(inverse[w]), split(last[w, 0:side, side:]), 1)
        column = jnp.concatenate([last[w, side:, 0:side], solved_v[w, :, 0:side]], 0)
        change = mul_split(split(column), split(held_u), 1)
        held[w, 0] = last[w, side : 2 * side, side:] - change[0:side]
        held[w, 1] = last[w, 2 * side :, side:] - change[side : 2 * side]
        held[w, 2] = solved_v[w, :, side:] - change[2 * side :]
        held[w, 3] = held_u


def whole_call(kernel, name, shapes, time, tiles=None, scratch=()):
    vmem = pl.BlockSpec(memory_space=pltpu.VMEM)

    def call(*args):
        specs = [vmem] * len(args)
        if tiles is not None:
            args = (*args, tiles)
            specs.append(pl.BlockSpec(memory_space=pl.ANY))
        return pl.pallas_call(
            kernel,
            name=name,
            out_shape=[jax.ShapeDtypeStruct(s, jnp.float32) for s in shapes],
            in_specs=specs,
            out_specs=[vmem] * len(shapes),
            scratch_shapes=list(scratch),
            compiler_params=pltpu.CompilerParams(vmem_limit_bytes=32 << 20),
            cost_estimate=pl.CostEstimate(flops=work(time), bytes_accessed=1 << 20, transcendentals=0),
        )(*args)

    return call


def split(x):
    high = x.astype(jnp.bfloat16)
    return high, (x - high.astype(jnp.float32)).astype(jnp.bfloat16)


def mul_split(a, b, along=0):
    dims = (((along,), (0,)), ((), ()))
    terms = [(a[0], b[0]), (a[0], b[1]), (a[1], b[0])]
    return sum(lax.dot_general(x, y, dims, preferred_element_type=jnp.float32) for x, y in terms)


MATE, CROSS, FAR = (0, 3), (2, 1), (2, 3)


def columns_kernel(side, groups, with_own, *refs):
    count = len(groups)
    if with_own:
        tiles, held, *arrays = refs[: 2 + count]
        out, coupling, diagonal, load_sems, buffer, sems = refs[2 + count :]
    else:
        _, held, *arrays = refs[: 2 + count]
        out, buffer, sems = refs[2 + count :]
    right, top = role()
    slots = {MATE: 2 * right + 1 - top, CROSS: 2 * (1 - right) + top, FAR: 2 * (1 - right) + 1 - top}
    waves = held.shape[0]
    inner, outer = (3 - top, 1 - right), (right, 2 + top)
    if with_own:
        loads = load_blocks(tiles, side, inner, outer, coupling, load_sems.at[0])
        loads += load_blocks(tiles, side, outer, outer, diagonal, load_sems.at[1])
    parts = {}

    def product(w, box, block):
        if (w, box) not in parts:
            parts[w, box] = split(jnp.concatenate([held[w, i] for i in box], 0))
        return mul_split(parts[w, box], split(block))

    stores = []

    def put(w, slot, j, value):
        n = len(stores)
        width = value.shape[1]
        buffer[n, :, 0:width] = value
        column = pl.multiple_of(slot * 2 * side + j * side, side)
        target = out.at[w, :, pl.ds(column, width)]
        stores.append(pltpu.make_async_copy(buffer.at[n, :, pl.ds(0, width)], target, sems.at[n]))
        stores[-1].start()

    for (box, units, base), array in zip(groups, arrays):
        n = 0
        while n < len(units):
            w, j = divmod(units[n], 2)
            pair = j == 0 and n + 1 < len(units) and units[n + 1] == units[n] + 1
            rows = [array[base + 2 * side * m : base + 2 * side * (m + 1), :] for m in range(n, n + 1 + pair)]
            block = jnp.concatenate(rows, 1)
            put(w, slots[box], j, -product(w, box, block))
            n += 2 if pair else 1
    if with_own:
        for load in loads:
            load.wait()
        for w in range(waves):
            put(w, 2 * right + top, 0, diagonal[w] - product(w, (0, 1), coupling[w]))
    for store in stores:
        store.wait()


def columns_call(name, time, source, held, pieces, with_own):
    waves, side = held.shape[0], held.shape[2]
    groups = tuple((box, units, base) for box, units, _, base in pieces)
    vmem, anywhere = pl.BlockSpec(memory_space=pltpu.VMEM), pl.BlockSpec(memory_space=pl.ANY)
    square = pltpu.VMEM((waves, 2 * side, 2 * side), jnp.float32)
    most = sum(len(units) for _, units, _, _ in pieces) + waves
    scratch = [pltpu.VMEM((most, 2 * side, 2 * side), jnp.float32), pltpu.SemaphoreType.DMA((most,))]
    if with_own:
        scratch = [square, square, pltpu.SemaphoreType.DMA((2, 4 * waves))] + scratch
    return pl.pallas_call(
        functools.partial(columns_kernel, side, groups, with_own),
        name=name,
        out_shape=jax.ShapeDtypeStruct((waves, 2 * side, 8 * side), jnp.float32),
        in_specs=[anywhere] + [vmem] * (1 + len(pieces)),
        out_specs=anywhere,
        scratch_shapes=scratch,
        input_output_aliases={} if with_own else {0: 0},
        compiler_params=pltpu.CompilerParams(vmem_limit_bytes=32 << 20),
        cost_estimate=pl.CostEstimate(flops=work(time), bytes_accessed=1 << 20, transcendentals=0),
    )(source, held, *(array for _, _, array, _ in pieces))


def body(children):
    tiles = children[:, 0, 0]
    waves, side = tiles.shape[0], tiles.shape[1] // 4
    units = tuple(range(2 * waves))
    first, second, third = units[:1], units[1:3], units[3:]
    base = waves * height(side)
    own, sent = packed(tiles, first)
    whole, part_1, part_2 = couplings(tiles, (units, second, third))
    cross_0 = swapped(sent, "gx")
    mate_pack = swapped(own, "gy")
    mate = swapped(whole, "gy")

    def eliminate(kernel, name, shapes, time, **more):
        shapes = [(waves, *shape) for shape in shapes]
        return whole_call(functools.partial(kernel, side), name, shapes, time, **more)

    full = 4 * side
    loads = [pltpu.VMEM((waves, 2 * side, 2 * side), jnp.float32), pltpu.SemaphoreType.DMA((4 * waves,))]
    solved_y, rest = eliminate(
        first_kernel, "eliminate_y", [(side, full), (2 * side, full)], 1, tiles=tiles, scratch=loads
    )(own, mate_pack)
    cross_1 = swapped(after(part_1, (cross_0, solved_y)), "gx")
    cross_2 = swapped(after(part_2, (cross_0, solved_y)), "gx")
    far_0 = swapped(cross_0, "gy")
    solved_x, left = eliminate(second_kernel, "eliminate_x", [(side, full), (3 * side, full)], 6)(
        cross_0, solved_y, rest
    )
    solved_v, last = eliminate(third_kernel, "eliminate_v", [(side, 3 * side), (3 * side, 3 * side)], 6)(
        far_0, solved_x, left
    )
    far_2 = swapped(after(cross_2, solved_v), "gy")
    far_1 = swapped(after(cross_1, solved_v), "gy")
    (held,) = eliminate(fourth_kernel, "eliminate_u", [(4, side, 2 * side)], 5)(solved_v, last)
    near = columns_call(
        "near_columns",
        3,
        tiles,
        held,
        [(MATE, units, mate, 0), (CROSS, first, cross_0, base), (FAR, first, far_0, base), (CROSS, second, cross_1, 0), (CROSS, third, cross_2, 0)],
        True,
    )
    merged = columns_call("last_columns", 1.5, near, held, [(FAR, third, far_2, 0), (FAR, second, far_1, 0)], False)
    return merged[:, None, None]


def solution(mesh):
    placed = (P("groups", "gx", "gy", None, None),)
    return jax.shard_map(
        body,
        mesh=mesh,
        in_specs=placed,
        out_specs=P("groups", "gx", "gy", None, None),
        check_vma=False,
    )
```
